32 devices in a mesh: leaf: 8 (over z, x), rhs: 4 (over y, core).
Axes of the slice: x: 2, y: 2, z: 4, core: 2. Of those that a mesh axis runs over, the one named last changes fastest.
Arguments:
- coords: bfloat16 [64, 32768], P(None, 'leaf'), may hold values from -1.5 to 1.5
- rhs: bfloat16 [256, 32768], P('rhs', 'leaf'), parts along dimension 0, may hold values from -6 to 6
- basis: bfloat16 [64, 512, 256], P('leaf'), may hold values from -0.25 to 0.25
- transfer_one: bfloat16 [32, 512, 256], P('leaf'), may hold values from -0.25 to 0.25
- transfer_two: bfloat16 [16, 512, 256], P('leaf'), may hold values from -0.25 to 0.25
- far_blocks: bfloat16 [112, 4, 256, 256], P('leaf'), may hold values from -0.375 to 0.375
- neighbours: int32 [64, 8], replicated, may hold values from 0 to 63, as said below
- far_lists: int32 [112, 4], replicated, may hold values from 0 to 111, as said below
Outputs:
- product: float32 [256, 32768], P('rhs', 'leaf'), parts along dimension 0
The draws below stay inside these ranges and needn't reach their ends.
There are 4 independent parts, one for each index of `rhs`. The reference program is written for one: setup_inputs(seed, part) draws one part's arguments, and reference() takes and returns one part's arrays. A program takes and returns all parts, laid end to end along the dimension named above; an argument that names none is the same for every part. Nothing has to cross between parts.
Inputs may be any that keep to these rules, and one draw needn't show every extreme that they name: `neighbours`: row i starts with leaf i itself; its other entries name leaves of other devices (leaf i lies on device i // 8). The entries after the first in the lists of one device's leaves name no other device more than 8 times, and the leaves of every device are named exactly 56 times by such entries over all lists. `far_lists`: entry (n, f) names a node of the same level as node n on another device (node n lies on device n // 14). The entries of one device's nodes name no other device more than 8 times, and the nodes of every device are named exactly 56 times over all entries.
All inputs are finite; a program needn't handle non-finite values.
Results may differ from the reference program's by a relative error of at most 0.005.
Values may be sent and summed in bfloat16 or wider, within the bound.
A program may use at most 128 MiB of HBM per device.

```python
import jax
import jax.numpy as jnp
from jax import lax

FEAT = 64
RANK = 256
R = 64
LEAF = 512
NB = 8
FAR = 4
LEAF_DEV = 8
LEAVES = 64
POINTS = 32768
NODE_DEV = 14
NODES = 112
N_LEAF = 8


def peer_targets(key, entry_count, peer_count):
    first_key, second_key = jax.random.split(key)
    placing = jax.random.permutation(first_key, peer_count).astype(jnp.int32)
    inverse = jnp.argsort(placing).astype(jnp.int32)
    offsets = (jax.random.permutation(second_key, peer_count - 1) + 1).astype(jnp.int32)
    chosen = offsets[jnp.arange(entry_count, dtype=jnp.int32) % (peer_count - 1)]
    devices = jnp.arange(peer_count, dtype=jnp.int32)
    return placing[(inverse[devices][:, None] + chosen[None, :]) % peer_count]


def draw_neighbours(key, part):
    peer_count = LEAVES // LEAF_DEV
    entry_count = (NB - 1) * LEAF_DEV
    first_key, second_key = jax.random.split(jax.random.fold_in(key, 11))
    owners = peer_targets(first_key, entry_count, peer_count)
    picked = jax.random.randint(second_key, (peer_count, entry_count), 0, LEAF_DEV, dtype=jnp.int32)
    remote = (owners * LEAF_DEV + picked).reshape(LEAVES, NB - 1)
    itself = jnp.arange(LEAVES, dtype=jnp.int32)[:, None]
    return jnp.concatenate([itself, remote], axis=1).astype(jnp.int32)


def draw_far_lists(key, part):
    peer_count = LEAVES // LEAF_DEV
    entry_count = NODE_DEV * FAR
    first_key, second_key = jax.random.split(jax.random.fold_in(key, 23))
    owners = peer_targets(first_key, entry_count, peer_count)
    asking = jnp.arange(entry_count, dtype=jnp.int32) // FAR
    level_start = jnp.where(asking < LEAF_DEV, 0, jnp.where(asking < LEAF_DEV * 3 // 2, LEAF_DEV, LEAF_DEV * 3 // 2))
    level_width = jnp.where(asking < LEAF_DEV, LEAF_DEV, jnp.where(asking < LEAF_DEV * 3 // 2, LEAF_DEV // 2, LEAF_DEV // 4))
    raw_pick = jax.random.randint(second_key, (peer_count, entry_count), 0, 1 << 20, dtype=jnp.int32)
    remote = owners * NODE_DEV + level_start[None, :] + raw_pick % level_width[None, :]
    return remote.reshape(NODES, FAR).astype(jnp.int32)


def level_of(own_key, dims, cuts, least, largest):
    level, own = 1.0, jax.random.fold_in(own_key, 6)
    for position, shards_of in cuts:
        draws = jnp.exp(jax.random.uniform(jax.random.fold_in(own, position), (shards_of,), jnp.float32, least / len(cuts), largest / len(cuts)))
        level = level * jnp.repeat(draws, dims[position] // shards_of).reshape([-1 if axis == position else 1 for axis in range(len(dims))])
    return level


def noise(stream_key, dims, scale, limit, cuts=(), kind=jnp.bfloat16):
    values = scale * jax.random.normal(stream_key, dims, jnp.float32)
    if cuts:
        values = values * level_of(stream_key, dims, cuts, -0.22, 0.18)
    return jnp.clip(values, -limit, limit).astype(kind)


def setup_inputs(seed: int = 0, part: int = 0) -> dict:
    splits = jax.random.split(jax.random.key(seed), 9)
    own_keys = jax.random.split(jax.random.fold_in(splits[8], part), 9)
    return {
        "coords": noise(splits[0], (FEAT, POINTS), 0.25, 1.5, ((1, 8),)),
        "rhs": noise(own_keys[1], (R, POINTS), 1.0, 6.0, ((1, 8),)),
        "basis": noise(splits[2], (LEAVES, LEAF, RANK), LEAF ** -0.5, 0.25, ((0, 8),)),
        "transfer_one": noise(splits[3], (LEAVES // 2, 2 * RANK, RANK), (2 * RANK) ** -0.5, 0.25, ((0, 8),)),
        "transfer_two": noise(splits[4], (LEAVES // 4, 2 * RANK, RANK), (2 * RANK) ** -0.5, 0.25, ((0, 8),)),
        "far_blocks": noise(splits[5], (NODES, FAR, RANK, RANK), RANK ** -0.5, 0.375, ((0, 8),)),
        "neighbours": draw_neighbours(jax.random.fold_in(splits[8], 71), part),
        "far_lists": draw_far_lists(jax.random.fold_in(splits[8], 71), part),
    }


def round_half(values):
    return lax.optimization_barrier(values.astype(jnp.bfloat16))


def kernel_tiles(sources, targets):
    src_f = sources.astype(jnp.float32)
    dst_f = targets.astype(jnp.float32)
    inner = jnp.einsum("...fa,...fb->...ab", src_f, dst_f, precision=lax.Precision.HIGHEST)
    src_sq = jnp.sum(src_f * src_f, axis=-2)
    dst_sq = jnp.sum(dst_f * dst_f, axis=-2)
    return round_half(jnp.exp(inner - 0.5 * src_sq[..., :, None] - 0.5 * dst_sq[..., None, :]))


def join_pairs(skeleton):
    return skeleton.reshape(-1, 2, R, RANK).transpose(0, 2, 1, 3).reshape(-1, R, 2 * RANK)


def descend(parent, transfer, child_far):
    rounded = round_half(parent).astype(jnp.float32)
    spread = jnp.einsum("mrk,mjk->mrj", rounded, transfer.astype(jnp.float32), precision=lax.Precision.HIGHEST)
    spread = spread.reshape(-1, R, 2, RANK).transpose(0, 2, 1, 3).reshape(-1, R, RANK)
    return child_far + spread


def reference(coords, rhs, basis, transfer_one, transfer_two, far_blocks, neighbours, far_lists):
    points = coords.reshape(FEAT, LEAVES, LEAF).transpose(1, 0, 2)
    charges = rhs.reshape(R, LEAVES, LEAF).transpose(1, 0, 2)

    def near_leaf(index):
        listed = neighbours[index]
        kernel = kernel_tiles(points[listed], points[index][None])
        return jnp.einsum("nra,nab->rb", charges[listed].astype(jnp.float32), kernel.astype(jnp.float32), precision=lax.Precision.HIGHEST)

    near = lax.map(near_leaf, jnp.arange(LEAVES, dtype=jnp.int32))
    skel_zero = round_half(jnp.einsum("lra,lak->lrk", charges.astype(jnp.float32), basis.astype(jnp.float32), precision=lax.Precision.HIGHEST))
    skel_one = round_half(jnp.einsum("mrj,mjk->mrk", join_pairs(skel_zero).astype(jnp.float32), transfer_one.astype(jnp.float32), precision=lax.Precision.HIGHEST))
    skel_two = round_half(jnp.einsum("mrj,mjk->mrk", join_pairs(skel_one).astype(jnp.float32), transfer_two.astype(jnp.float32), precision=lax.Precision.HIGHEST))
    skeleton = jnp.concatenate([
        skel_zero.reshape(N_LEAF, LEAF_DEV, R, RANK),
        skel_one.reshape(N_LEAF, LEAF_DEV // 2, R, RANK),
        skel_two.reshape(N_LEAF, LEAF_DEV // 4, R, RANK)], axis=1).reshape(NODES, R, RANK)
    far = jnp.zeros((NODES, R, RANK), jnp.float32)
    for partner in range(FAR):
        weights = skeleton[far_lists[:, partner]].astype(jnp.float32)
        far = far + jnp.einsum("nrk,nkj->nrj", weights, far_blocks[:, partner].astype(jnp.float32), precision=lax.Precision.HIGHEST)
    far = far.reshape(N_LEAF, NODE_DEV, R, RANK)
    far_zero = far[:, :LEAF_DEV].reshape(LEAVES, R, RANK)
    far_one = far[:, LEAF_DEV:LEAF_DEV * 3 // 2].reshape(LEAVES // 2, R, RANK)
    far_two = far[:, LEAF_DEV * 3 // 2:].reshape(LEAVES // 4, R, RANK)
    middle = descend(far_two, transfer_two, far_one)
    lowest = descend(middle, transfer_one, far_zero)
    lowest_rounded = round_half(lowest).astype(jnp.float32)
    result = near + jnp.einsum("lrk,lak->lra", lowest_rounded, basis.astype(jnp.float32), precision=lax.Precision.HIGHEST)
    return result.transpose(1, 0, 2).reshape(R, POINTS)
```

```python
import functools

import jax
import jax.numpy as jnp
from jax import lax
from jax.experimental import pallas as pl
from jax.experimental.pallas import tpu as pltpu
from jax.sharding import PartitionSpec as P

FEAT = 64
RANK = 256
R = 64
LEAF = 512
NB = 8
FAR = 4


def kernel_tiles(sources, targets):
    inner = jnp.einsum("...fa,...fb->...ab", sources, targets, preferred_element_type=jnp.float32)
    src_f = sources.astype(jnp.float32)
    dst_f = targets.astype(jnp.float32)
    src_sq = jnp.sum(src_f * src_f, axis=-2)
    dst_sq = jnp.sum(dst_f * dst_f, axis=-2)
    return jnp.exp(inner - 0.5 * src_sq[..., :, None] - 0.5 * dst_sq[..., None, :]).astype(
        jnp.bfloat16
    )


def tile_products(sources, targets):
    kernel = kernel_tiles(sources[:, :FEAT], targets)
    return jnp.einsum("gra,gab->grb", sources[:, FEAT:], kernel, preferred_element_type=jnp.float32)


def grouped_products(sources, targets):
    groups = sources.shape[0] // 4
    paired = (
        sources.reshape(groups, 4, sources.shape[1], sources.shape[2]),
        targets.reshape(groups, 4, targets.shape[1], targets.shape[2]),
    )
    outcome = lax.map(lambda couple: tile_products(couple[0], couple[1]), paired)
    return outcome.reshape(sources.shape[0], R, sources.shape[2])


def slot_ranks(owners):
    entry_count = owners.shape[1]
    position = jnp.arange(entry_count, dtype=jnp.int32)
    earlier = position[None, :] < position[:, None]
    matches = owners[:, :, None] == owners[:, None, :]
    return jnp.sum(jnp.logical_and(matches, earlier[None]), axis=2)


def wanted_entries(owners, ranks, entries, device_index, slot_count):
    slots = jnp.arange(slot_count, dtype=jnp.int32)
    taken = (owners == device_index)[:, None, :] & (ranks[:, None, :] == slots[:, None])
    return jnp.sum(jnp.where(taken, entries[:, None, :], 0), axis=2).reshape(-1)


def select(items, indices):
    taken = (indices[:, None] == jnp.arange(items.shape[0], dtype=jnp.int32)).astype(items.dtype)
    return jnp.einsum("sn,nrk->srk", taken, items, preferred_element_type=jnp.float32).astype(items.dtype)


def join_pairs(skeleton):
    return skeleton.reshape(-1, 2, R, RANK).transpose(0, 2, 1, 3).reshape(-1, R, 2 * RANK)


def descend(parent, transfer, child_far):
    rounded = parent.astype(jnp.bfloat16)
    spread = jnp.einsum("mrk,mjk->mrj", rounded, transfer, preferred_element_type=jnp.float32)
    spread = spread.reshape(-1, R, 2, RANK).transpose(0, 2, 1, 3).reshape(-1, R, RANK)
    return child_far + spread


def exchanged(coords, rhs, basis, transfer_one, transfer_two, far_blocks, neighbours, far_lists):
    peer_count = lax.axis_size("leaf")
    device_index = lax.axis_index("leaf")
    local_leaves = basis.shape[0]
    node_count = far_blocks.shape[0]
    remote_count = (NB - 1) * local_leaves
    near_slots = (remote_count + peer_count - 2) // (peer_count - 1)
    far_count = node_count * FAR
    far_slots = (far_count + peer_count - 2) // (peer_count - 1)
    points = coords.reshape(FEAT, local_leaves, LEAF).transpose(1, 0, 2)
    charges = rhs.reshape(R, local_leaves, LEAF).transpose(1, 0, 2)
    blocks = jnp.concatenate([points, charges], axis=1)
    remote = neighbours.reshape(peer_count, local_leaves, NB)[:, :, 1:].reshape(
        peer_count, remote_count
    )
    owners = remote // local_leaves
    ranks = slot_ranks(owners)
    my_owners = lax.dynamic_index_in_dim(owners, device_index, 0, keepdims=False)
    my_ranks = lax.dynamic_index_in_dim(ranks, device_index, 0, keepdims=False)
    my_slots = my_owners * near_slots + my_ranks
    wanted = wanted_entries(owners, ranks, remote, device_index, near_slots)
    skel_zero = jnp.einsum(
        "lra,lak->lrk", charges, basis, preferred_element_type=jnp.float32
    ).astype(jnp.bfloat16)
    skel_one = jnp.einsum(
        "mrj,mjk->mrk", join_pairs(skel_zero), transfer_one, preferred_element_type=jnp.float32
    ).astype(jnp.bfloat16)
    skel_two = jnp.einsum(
        "mrj,mjk->mrk", join_pairs(skel_one), transfer_two, preferred_element_type=jnp.float32
    ).astype(jnp.bfloat16)
    skeleton = jnp.concatenate([skel_zero, skel_one, skel_two], axis=0)
    far_remote = far_lists.reshape(peer_count, far_count)
    far_owners = far_remote // node_count
    far_ranks = slot_ranks(far_owners)
    far_wanted = wanted_entries(far_owners, far_ranks, far_remote, device_index, far_slots)
    far_buffer = select(skeleton, far_wanted % node_count)
    far_arrived = lax.all_to_all(
        far_buffer.reshape(peer_count, far_slots, R, RANK),
        "leaf",
        split_axis=0,
        concat_axis=0,
        tiled=True,
    )
    my_far = lax.dynamic_index_in_dim(
        far_owners, device_index, 0, keepdims=False
    ) * far_slots + lax.dynamic_index_in_dim(far_ranks, device_index, 0, keepdims=False)
    partners = select(far_arrived.reshape(peer_count * far_slots, R, RANK), my_far).reshape(
        node_count, FAR, R, RANK
    )
    leaf_buffer = select(blocks, wanted % local_leaves)
    leaf_arrived = lax.all_to_all(
        leaf_buffer.reshape(peer_count, near_slots, FEAT + R, LEAF),
        "leaf",
        split_axis=0,
        concat_axis=0,
        tiled=True,
    )
    sources = select(leaf_arrived.reshape(peer_count * near_slots, FEAT + R, LEAF), my_slots)
    per_item = grouped_products(sources, jnp.repeat(points, NB - 1, axis=0))
    self_terms = tile_products(blocks, points)
    near = self_terms + jnp.sum(per_item.reshape(local_leaves, NB - 1, R, LEAF), axis=1)
    far = jnp.einsum("nfrk,nfkj->nrj", partners, far_blocks, preferred_element_type=jnp.float32)
    far_zero = far[:local_leaves]
    far_one = far[local_leaves : local_leaves * 3 // 2]
    far_two = far[local_leaves * 3 // 2 :]
    middle = descend(far_two, transfer_two, far_one)
    lowest = descend(middle, transfer_one, far_zero)
    result = near + jnp.einsum(
        "lrk,lak->lra", lowest.astype(jnp.bfloat16), basis, preferred_element_type=jnp.float32
    )
    return result.transpose(1, 0, 2).reshape(R, local_leaves * LEAF)


AUG = 16
CHUNK = 2
UNROLL = 4


def half_square_terms(points):
    points_f = points.astype(jnp.float32)
    half = -0.5 * jnp.sum(points_f * points_f, axis=0, keepdims=True)
    high = half.astype(jnp.bfloat16).astype(jnp.float32)
    rest = half - high
    middle = rest.astype(jnp.bfloat16).astype(jnp.float32)
    return high, middle, rest - middle


def extra_rows(points, first):
    shape = (AUG, points.shape[1])
    line = lax.broadcasted_iota(jnp.int32, shape, 0)
    ones = jnp.logical_and(line >= 3 - first, line < 6 - first)
    rows = jnp.where(ones, 1.0, 0.0)
    for at, term in enumerate(half_square_terms(points)):
        rows = jnp.where(line == first + at, jnp.broadcast_to(term, shape), rows)
    return rows.astype(jnp.bfloat16)


def tile(source, target, charge):
    exponent = lax.dot_general(
        source, target, (((0,), (0,)), ((), ())), preferred_element_type=jnp.float32
    )
    return jnp.dot(charge, jnp.exp(exponent).astype(jnp.bfloat16), preferred_element_type=jnp.float32)


def target_orders(rows):
    def key(at):
        return lambda row: (abs(row - at), abs(2 * row - rows + 1))

    return [sorted((row for row in range(rows) if row != at), key=key(at)) for at in range(rows)]


def whole_kernel(
    rows, parts, near, ends, far, coords_hbm, rhs_hbm, basis_hbm, one_hbm, two_hbm, blocks_hbm, out,
    own_points, across_points, points, own_charges, across_charges, skel, given, far_across,
    sums_out, sums_in, sources, targets, charges, skel_work, terms, far_out, far_at,
    basis, one, two, blocks,
    load_sem, leaf_sem, point_send, point_recv, peer_send, peer_recv, skel_send, skel_recv,
    sum_send, sum_recv, cross_send, cross_recv, given_send, given_recv,
):
    leaves, nodes = basis.shape[0], skel.shape[1]
    share = FEAT // parts
    chunks = leaves // CHUNK
    leaf, part = lax.axis_index("leaf"), lax.axis_index("rhs")
    row, side = leaf // 2, leaf % 2
    across = (row * 2 + 1 - side, part)
    mesh_ids = pl.DeviceIdType.MESH
    orders = target_orders(rows)

    def by_row(values):
        total = 0
        for at, value in enumerate(values):
            off = (row - at + rows) % rows
            total = total + value * (1 - (off + rows - 1) // rows)
        return total

    far_targets = [by_row([orders[at][k] for at in range(rows)]) for k in range(rows - 1)]
    ways = [by_row([int(orders[at][k] < at) for at in range(rows)]) for k in range(rows - 1)]

    loads = [
        pltpu.make_async_copy(source, target, load_sem.at[which])
        for which, (source, target) in enumerate(
            ((basis_hbm, basis), (one_hbm, one), (two_hbm, two), (blocks_hbm, blocks))
        )
    ]
    leaf_loads = [
        pltpu.make_async_copy(
            source.at[:, pl.ds(index * LEAF, LEAF)], target.at[index], leaf_sem.at[which, index]
        )
        for which, (source, target) in enumerate(
            ((coords_hbm, own_points), (rhs_hbm, own_charges))
        )
        for index in range(leaves)
    ]
    for load in leaf_loads + loads:
        load.start()

    barrier = pltpu.get_barrier_semaphore()
    partners = [across] + [(leaf, (part + away) % parts) for away in range(1, parts)]
    for partner in partners:
        pl.semaphore_signal(barrier, inc=1, device_id=partner, device_id_type=mesh_ids)

    @pl.when(row > 0)
    def _():
        pl.semaphore_signal(barrier, inc=1, device_id=(leaf - 2, part), device_id_type=mesh_ids)

    @pl.when(row < rows - 1)
    def _():
        pl.semaphore_signal(barrier, inc=1, device_id=(leaf + 2, part), device_id_type=mesh_ids)

    ahead = (row + rows - 1) // rows + (2 * rows - 2 - row) // rows
    pl.semaphore_wait(barrier, len(partners) + ahead)

    def remote(source, target, send, recv, device):
        return pltpu.make_async_remote_copy(
            src_ref=source, dst_ref=target, send_sem=send, recv_sem=recv,
            device_id=device, device_id_type=mesh_ids,
        )

    def neighbour(way):
        return (leaf + 2 - 4 * way, part)

    my_share = pl.ds(pl.multiple_of(part * share, share), share)

    def point_hop(origin, way, own=False):
        source = own_points.at[:, my_share, :] if own else points.at[origin, :, my_share, :]
        return remote(
            source, points.at[origin, :, my_share, :], point_send.at[origin, way],
            point_recv.at[origin], neighbour(way),
        )

    skel_parts = (pl.ds(0, leaves), pl.ds(leaves, nodes - leaves))

    def skel_hop(origin, way, piece):
        held = skel.at[origin, skel_parts[piece]]
        return remote(
            held, held, skel_send.at[origin, piece, way], skel_recv.at[origin, piece],
            neighbour(way),
        )

    def cross(which):
        if which == 0:
            source, target = own_points.at[:, my_share, :], across_points.at[:, my_share, :]
        else:
            source, target = own_charges, across_charges
        return remote(source, target, cross_send.at[which], cross_recv.at[which], across)

    def given_hop(origin):
        return remote(
            given.at[origin], far_across.at[origin], given_send.at[origin],
            given_recv.at[origin], across,
        )

    def to_peer(unit, away):
        if unit is None:
            held, at = across_points.at[:, my_share, :], rows
        else:
            held, at = points.at[unit, :, my_share, :], unit
        return remote(
            held, held, peer_send.at[at, away - 1], peer_recv.at[at, away - 1],
            (leaf, (part + away) % parts),
        )

    def share_points(unit):
        for away in range(1, parts):
            to_peer(unit, away).start()

    def shared(unit):
        for away in range(1, parts):
            to_peer(unit, away).wait_recv()

    def sum_hop(target, way, chunk):
        span = pl.ds(chunk * CHUNK, CHUNK)
        return remote(
            sums_out.at[target, span], sums_in.at[way, target, span], sum_send.at[target, chunk],
            sum_recv.at[way, target, chunk], neighbour(way),
        )

    def flow(distance, arrive, onward):
        @pl.when(row >= distance)
        def _():
            origin = row - distance
            if distance:
                arrive(origin)

            @pl.when(row < rows - 1)
            def _():
                onward(origin, 0)

        @pl.when(row + distance < rows)
        def _():
            origin = row + distance
            if distance:
                arrive(origin)

            @pl.when(row > 0)
            def _():
                onward(origin, 1)

    def at_distance(distance, action):
        pl.when(row >= distance)(lambda: action(row - distance))
        pl.when(row + distance < rows)(lambda: action(row + distance))

    def relay_points(distance):
        flow(
            distance,
            lambda origin: point_hop(origin, 0).wait_recv(),
            lambda origin, way: point_hop(origin, way, distance == 0).start(),
        )
        if distance:
            at_distance(distance, share_points)

    def relay_skel(distance, piece):
        flow(
            distance,
            lambda origin: skel_hop(origin, 0, piece).wait_recv(),
            lambda origin, way: skel_hop(origin, way, piece).start(),
        )

    def fill(unit, from_points):
        for index in range(leaves):
            taken = from_points(index)
            targets[unit * leaves + index, :FEAT] = taken
            targets[unit * leaves + index, FEAT:] = extra_rows(taken, 3)

    def fill_sources(first, from_points, from_charges):
        for index in range(leaves):
            taken = from_points[index]
            sources[first + index, :FEAT] = taken
            sources[first + index, FEAT:] = extra_rows(taken, 0)
            charges[first + index] = from_charges[index]

    def run_tiles(place):
        def entry(index, carry):
            at = place * leaves + index
            source = near[0, at]
            term = tile(sources[source], targets[near[1, at]], charges[source])
            kept = jnp.where(near[2, at] == 1, 0.0, terms[at])
            terms[at + 1] = kept + term
            return carry

        lax.fori_loop(0, leaves, entry, 0, unroll=UNROLL)

    def near_sum(target, index):
        at = target * leaves + index
        return terms[ends[0, at]] + terms[ends[1, at]]

    def edge_sums(k):
        target, way = far_targets[k], ways[k]

        def send():
            for chunk in range(chunks):
                for index in range(chunk * CHUNK, (chunk + 1) * CHUNK):
                    sums_out[target, index] = near_sum(target, index).astype(jnp.bfloat16)
                sum_hop(target, way, chunk).start()

        pl.when(jnp.logical_or(row == 0, row == rows - 1))(send)

    def inner_sums(k, chunk):
        target, way = far_targets[k], ways[k]

        def send():
            sum_hop(target, way, chunk).wait_recv()
            for index in range(chunk * CHUNK, (chunk + 1) * CHUNK):
                arrived = sums_in[way, target, index].astype(jnp.float32)
                sums_out[target, index] = (near_sum(target, index) + arrived).astype(jnp.bfloat16)
            sum_hop(target, way, chunk).start()

        pl.when(jnp.logical_and(row > 0, row < rows - 1))(send)

    def far_product(weights, at):
        far_out[at] = jnp.dot(weights, blocks[far[1, at]], preferred_element_type=jnp.float32)

    def give(origin):
        skel_work[...] = skel[origin]
        for index in range(leaves):
            given[origin, index] = skel_work[far[3, origin * leaves + index]]
        given_hop(origin).start()

    def far_own(origin):
        give(origin)

        def entry(index, carry):
            at = origin * leaves + index
            far_product(skel_work[far[0, at]], at)
            return carry

        lax.fori_loop(0, leaves, entry, 0, unroll=UNROLL)

    def far_beside(origin):
        given_hop(origin).wait_recv()

        def entry(index, carry):
            far_product(far_across[origin, index], (rows + origin) * leaves + index)
            return carry

        lax.fori_loop(0, leaves, entry, 0, unroll=UNROLL)

    for load in leaf_loads:
        load.wait()
    relay_points(0)
    cross(0).start()
    cross(1).start()
    terms[0] = jnp.zeros_like(terms[0])
    fill_sources(0, own_points, own_charges)
    fill(row, lambda index: own_points[index])

    for load in loads[:3]:
        load.wait()
    first_one, first_two = leaves, leaves * 3 // 2

    def joined(first, transfer):
        left = jnp.dot(skel[row, first], transfer[:RANK], preferred_element_type=jnp.float32)
        right = jnp.dot(skel[row, first + 1], transfer[RANK:], preferred_element_type=jnp.float32)
        return (left + right).astype(jnp.bfloat16)

    for index in range(leaves):
        skel[row, index] = jnp.dot(
            own_charges[index], basis[index], preferred_element_type=jnp.float32
        ).astype(jnp.bfloat16)
    relay_skel(0, 0)
    for index in range(first_two - first_one):
        skel[row, first_one + index] = joined(2 * index, one[index])
    for index in range(nodes - first_two):
        skel[row, first_two + index] = joined(first_one + 2 * index, two[index])
    relay_skel(0, 1)
    give(row)

    relay_points(1)
    cross(0).wait_recv()
    share_points(None)
    run_tiles(row)
    relay_points(2)
    near_first = far_targets[0]
    shared(near_first)
    fill(near_first, lambda index: points[near_first, index])
    run_tiles(near_first)
    for distance in range(3, rows):
        relay_points(distance)
    relay_skel(1, 0)
    for k in range(1, rows - 1):
        target = far_targets[k]
        shared(target)
        fill(target, lambda index: points[target, index])
        if k == 1:
            run_tiles(target)
    relay_skel(1, 1)
    run_tiles(far_targets[rows - 2])
    loads[3].wait()
    at_distance(1, far_own)
    shared(None)
    cross(1).wait_recv()
    fill_sources(leaves, across_points, across_charges)
    for k in reversed(range(rows - 1)):
        run_tiles(rows + far_targets[k])
        edge_sums(k)
        if k == 1:
            relay_skel(2, 0)
    run_tiles(rows + row)
    relay_skel(2, 1)
    at_distance(2, far_own)
    for chunk in range(chunks):
        inner_sums(rows - 2, chunk)
    far_beside(row)
    at_distance(1, far_beside)
    for chunk in range(chunks):
        inner_sums(1, chunk)
    for distance in range(3, rows):
        for piece in range(2):
            relay_skel(distance, piece)
        at_distance(distance, far_own)
    at_distance(2, far_beside)
    for chunk in range(chunks):
        inner_sums(0, chunk)
    for distance in range(3, rows):
        at_distance(distance, far_beside)

    for node in range(nodes):
        total = far_out[far[2, node * FAR]]
        for partner in range(1, FAR):
            total = total + far_out[far[2, node * FAR + partner]]
        far_at[node] = total

    def spread_to(parent, transfer):
        return lax.dot_general(
            parent.astype(jnp.bfloat16), transfer, (((1,), (1,)), ((), ())),
            preferred_element_type=jnp.float32,
        )

    for parent in range(nodes - first_two):
        spread = spread_to(far_at[first_two + parent], two[parent])
        for child in range(2):
            far_at[first_one + 2 * parent + child] += spread[:, child * RANK : (child + 1) * RANK]
    for parent in range(first_two - first_one):
        spread = spread_to(far_at[first_one + parent], one[parent])
        for child in range(2):
            far_at[2 * parent + child] += spread[:, child * RANK : (child + 1) * RANK]
    for index in range(leaves):
        out[:, index * LEAF : (index + 1) * LEAF] = near_sum(row, index) + spread_to(
            far_at[index], basis[index]
        )

    def add_arrived(way, chunk):
        sum_hop(row, way, chunk).wait_recv()
        for index in range(chunk * CHUNK, (chunk + 1) * CHUNK):
            span = slice(index * LEAF, (index + 1) * LEAF)
            out[:, span] += sums_in[way, row, index].astype(jnp.float32)

    for chunk in range(chunks):
        pl.when(row > 0)(functools.partial(add_arrived, 0, chunk))
        pl.when(row < rows - 1)(functools.partial(add_arrived, 1, chunk))

    for distance in range(rows):
        flow(
            distance,
            lambda origin: None,
            lambda origin, way: point_hop(origin, way, distance == 0).wait_send(),
        )
        for piece in range(2):
            flow(
                distance,
                lambda origin: None,
                lambda origin, way: skel_hop(origin, way, piece).wait_send(),
            )
    for which in range(2):
        cross(which).wait_send()
    for origin in range(rows):
        given_hop(origin).wait_send()
    for away in range(1, parts):
        to_peer(None, away).wait_send()
        for k in range(rows - 1):
            to_peer(far_targets[k], away).wait_send()
    for k in range(rows - 1):
        for chunk in range(chunks):
            sum_hop(far_targets[k], ways[k], chunk).wait_send()


def on_device(coords, rhs, basis, transfer_one, transfer_two, far_blocks, neighbours, far_lists):
    peer_count = lax.axis_size("leaf")
    whole_lists = peer_count == NB and peer_count % 2 == 0
    even_lists = far_blocks.shape[0] * FAR == (NB - 1) * basis.shape[0]
    even_shares = FEAT % lax.axis_size("rhs") == 0
    route = gathered if whole_lists and even_lists and even_shares else exchanged
    return route(coords, rhs, basis, transfer_one, transfer_two, far_blocks, neighbours, far_lists)


def chosen_entries(matches, ranks, values, count):
    slots = jnp.arange(count, dtype=jnp.int32)
    taken = matches[..., None, :] & (ranks[..., None, :] == slots[:, None])
    return jnp.sum(jnp.where(taken, values[..., None, :], 0), axis=-1)


def route_tables(rows, leaves, nodes, row, side, neighbours, far_lists):
    listed = leaves * NB
    column = lax.dynamic_index_in_dim(neighbours.reshape(rows, 2, listed), side, 1, keepdims=False)
    own = jnp.stack([row * 2 + side, row * 2 + 1 - side])
    matches = (column // leaves)[None] == own[:, None, None]
    position = jnp.arange(listed, dtype=jnp.int32)
    earlier = position[None, :] < position[:, None]
    same_leaf = position[None, :] // NB == position[:, None] // NB
    counted = matches[:, :, None, :]
    ranks = jnp.sum(counted & earlier, axis=3, dtype=jnp.int32)
    opens = jnp.sum(counted & earlier & same_leaf, axis=3, dtype=jnp.int32) == 0
    source = jnp.arange(2, dtype=jnp.int32)[:, None, None] * leaves + (column % leaves)[None]
    target = jnp.arange(rows, dtype=jnp.int32)[:, None] * leaves + position // NB
    values = (source * (rows * leaves) + target) * 2 + opens
    picked = chosen_entries(matches, ranks, values, leaves).reshape(-1)
    near = jnp.stack([picked // (2 * rows * leaves), picked // 2 % (rows * leaves), picked % 2])
    leaf_of = position // NB
    leaf_ids = jnp.arange(leaves, dtype=jnp.int32)[:, None]
    upto = jnp.sum(counted & (leaf_of <= leaf_ids), axis=3, dtype=jnp.int32)
    some = jnp.any(counted & (leaf_of == leaf_ids), axis=3)
    places = jnp.arange(2 * rows, dtype=jnp.int32).reshape(2, rows, 1) * leaves
    ends = jnp.where(some, places + upto, 0).reshape(2, rows * leaves)

    count = nodes * FAR
    peers = far_lists.reshape(rows, 2, count)
    pair = lax.dynamic_index_in_dim(peers, row, 0, keepdims=False)
    mine = lax.dynamic_index_in_dim(pair, side, 0, keepdims=False)
    beside = lax.dynamic_index_in_dim(pair, 1 - side, 0, keepdims=False)
    lists = jnp.stack([mine, beside])
    sides = jnp.stack([side, 1 - side])[:, None]
    owners = lists // nodes
    slot = (owners + sides) % 2 * rows + owners // 2
    entry = jnp.arange(count, dtype=jnp.int32)
    before = entry[None, :] < entry[:, None]
    rank = jnp.sum((slot[:, :, None] == slot[:, None, :]) & before, axis=2, dtype=jnp.int32)
    place = slot * leaves + rank
    wide = 2 * rows * leaves
    chosen = chosen_entries(jnp.full((2, count), True), place, lists % nodes * count + entry, wide)
    far = jnp.stack(
        [
            chosen[0] // count,
            chosen[0] % count,
            jnp.pad(place[0], (0, wide - count)),
            jnp.roll(chosen[1] // count, -rows * leaves),
        ]
    )
    return near, ends, far


def gathered(coords, rhs, basis, transfer_one, transfer_two, far_blocks, neighbours, far_lists):
    peer_count = lax.axis_size("leaf")
    parts = lax.axis_size("rhs")
    rows = peer_count // 2
    device_index = lax.axis_index("leaf")
    leaves, nodes = basis.shape[0], far_blocks.shape[0]
    tables = route_tables(
        rows, leaves, nodes, device_index // 2, device_index % 2, neighbours, far_lists
    )
    smem = pl.BlockSpec(memory_space=pltpu.SMEM)
    anywhere = pl.BlockSpec(memory_space=pl.ANY)
    bf16, f32 = jnp.bfloat16, jnp.float32
    chunks = leaves // CHUNK
    dma = pltpu.SemaphoreType.DMA
    return pl.pallas_call(
        functools.partial(whole_kernel, rows, parts),
        out_shape=jax.ShapeDtypeStruct((R, rhs.shape[1]), f32),
        in_specs=[smem] * 3 + [anywhere] * 6,
        out_specs=pl.BlockSpec(memory_space=pltpu.VMEM),
        scratch_shapes=[
            pltpu.VMEM((leaves, FEAT, LEAF), bf16),
            pltpu.VMEM((leaves, FEAT, LEAF), bf16),
            pltpu.VMEM((rows, leaves, FEAT, LEAF), bf16),
            pltpu.VMEM((leaves, R, LEAF), bf16),
            pltpu.VMEM((leaves, R, LEAF), bf16),
            pltpu.VMEM((rows, nodes, R, RANK), bf16),
            pltpu.VMEM((rows, leaves, R, RANK), bf16),
            pltpu.VMEM((rows, leaves, R, RANK), bf16),
            pltpu.VMEM((rows, leaves, R, LEAF), bf16),
            pltpu.VMEM((2, rows, leaves, R, LEAF), bf16),
            pltpu.VMEM((2 * leaves, FEAT + AUG, LEAF), bf16),
            pltpu.VMEM((rows * leaves, FEAT + AUG, LEAF), bf16),
            pltpu.VMEM((2 * leaves, R, LEAF), bf16),
            pltpu.VMEM((nodes, R, RANK), bf16),
            pltpu.VMEM((peer_count * leaves + 1, R, LEAF), f32),
            pltpu.VMEM((peer_count * leaves, R, RANK), f32),
            pltpu.VMEM((nodes, R, RANK), f32),
            pltpu.VMEM(basis.shape, bf16),
            pltpu.VMEM(transfer_one.shape, bf16),
            pltpu.VMEM(transfer_two.shape, bf16),
            pltpu.VMEM((nodes * FAR, RANK, RANK), bf16),
            dma((4,)),
            dma((2, leaves)),
            dma((rows, 2)),
            dma((rows,)),
            dma((rows + 1, parts - 1)),
            dma((rows + 1, parts - 1)),
            dma((rows, 2, 2)),
            dma((rows, 2)),
            dma((rows, chunks)),
            dma((2, rows, chunks)),
            dma((2,)),
            dma((2,)),
            dma((rows,)),
            dma((rows,)),
        ],
        compiler_params=pltpu.CompilerParams(
            collective_id=0, has_side_effects=True, vmem_limit_bytes=60 * 1024 * 1024
        ),
        name="whole",
    )(
        *tables, coords, rhs, basis, transfer_one, transfer_two,
        far_blocks.reshape(nodes * FAR, RANK, RANK),
    )


def solution(mesh):
    return jax.shard_map(
        on_device,
        mesh=mesh,
        in_specs=(
            P(None, "leaf"),
            P("rhs", "leaf"),
            P("leaf", None, None),
            P("leaf", None, None),
            P("leaf", None, None),
            P("leaf", None, None, None),
            P(),
            P(),
        ),
        out_specs=P("rhs", "leaf"),
        check_vma=False,
    )
```

```python
import functools

import jax
import jax.numpy as jnp
from jax import lax
from jax.experimental import pallas as pl
from jax.experimental.pallas import tpu as pltpu
from jax.sharding import PartitionSpec as P

FEAT = 64
RANK = 256
R = 64
LEAF = 512
NB = 8
FAR = 4


def kernel_tiles(sources, targets):
    inner = jnp.einsum("...fa,...fb->...ab", sources, targets, preferred_element_type=jnp.float32)
    src_f = sources.astype(jnp.float32)
    dst_f = targets.astype(jnp.float32)
    src_sq = jnp.sum(src_f * src_f, axis=-2)
    dst_sq = jnp.sum(dst_f * dst_f, axis=-2)
    return jnp.exp(inner - 0.5 * src_sq[..., :, None] - 0.5 * dst_sq[..., None, :]).astype(
        jnp.bfloat16
    )


def tile_products(sources, targets):
    kernel = kernel_tiles(sources[:, :FEAT], targets)
    return jnp.einsum("gra,gab->grb", sources[:, FEAT:], kernel, preferred_element_type=jnp.float32)


def grouped_products(sources, targets):
    groups = sources.shape[0] // 4
    paired = (
        sources.reshape(groups, 4, sources.shape[1], sources.shape[2]),
        targets.reshape(groups, 4, targets.shape[1], targets.shape[2]),
    )
    outcome = lax.map(lambda couple: tile_products(couple[0], couple[1]), paired)
    return outcome.reshape(sources.shape[0], R, sources.shape[2])


def slot_ranks(owners):
    entry_count = owners.shape[1]
    position = jnp.arange(entry_count, dtype=jnp.int32)
    earlier = position[None, :] < position[:, None]
    matches = owners[:, :, None] == owners[:, None, :]
    return jnp.sum(jnp.logical_and(matches, earlier[None]), axis=2)


def wanted_entries(owners, ranks, entries, device_index, slot_count):
    slots = jnp.arange(slot_count, dtype=jnp.int32)
    taken = (owners == device_index)[:, None, :] & (ranks[:, None, :] == slots[:, None])
    return jnp.sum(jnp.where(taken, entries[:, None, :], 0), axis=2).reshape(-1)


def select(items, indices):
    taken = (indices[:, None] == jnp.arange(items.shape[0], dtype=jnp.int32)).astype(items.dtype)
    return jnp.einsum("sn,nrk->srk", taken, items, preferred_element_type=jnp.float32).astype(items.dtype)


def join_pairs(skeleton):
    return skeleton.reshape(-1, 2, R, RANK).transpose(0, 2, 1, 3).reshape(-1, R, 2 * RANK)


def descend(parent, transfer, child_far):
    rounded = parent.astype(jnp.bfloat16)
    spread = jnp.einsum("mrk,mjk->mrj", rounded, transfer, preferred_element_type=jnp.float32)
    spread = spread.reshape(-1, R, 2, RANK).transpose(0, 2, 1, 3).reshape(-1, R, RANK)
    return child_far + spread


def exchanged(coords, rhs, basis, transfer_one, transfer_two, far_blocks, neighbours, far_lists):
    peer_count = lax.axis_size("leaf")
    device_index = lax.axis_index("leaf")
    local_leaves = basis.shape[0]
    node_count = far_blocks.shape[0]
    remote_count = (NB - 1) * local_leaves
    near_slots = (remote_count + peer_count - 2) // (peer_count - 1)
    far_count = node_count * FAR
    far_slots = (far_count + peer_count - 2) // (peer_count - 1)
    points = coords.reshape(FEAT, local_leaves, LEAF).transpose(1, 0, 2)
    charges = rhs.reshape(R, local_leaves, LEAF).transpose(1, 0, 2)
    blocks = jnp.concatenate([points, charges], axis=1)
    remote = neighbours.reshape(peer_count, local_leaves, NB)[:, :, 1:].reshape(
        peer_count, remote_count
    )
    owners = remote // local_leaves
    ranks = slot_ranks(owners)
    my_owners = lax.dynamic_index_in_dim(owners, device_index, 0, keepdims=False)
    my_ranks = lax.dynamic_index_in_dim(ranks, device_index, 0, keepdims=False)
    my_slots = my_owners * near_slots + my_ranks
    wanted = wanted_entries(owners, ranks, remote, device_index, near_slots)
    skel_zero = jnp.einsum(
        "lra,lak->lrk", charges, basis, preferred_element_type=jnp.float32
    ).astype(jnp.bfloat16)
    skel_one = jnp.einsum(
        "mrj,mjk->mrk", join_pairs(skel_zero), transfer_one, preferred_element_type=jnp.float32
    ).astype(jnp.bfloat16)
    skel_two = jnp.einsum(
        "mrj,mjk->mrk", join_pairs(skel_one), transfer_two, preferred_element_type=jnp.float32
    ).astype(jnp.bfloat16)
    skeleton = jnp.concatenate([skel_zero, skel_one, skel_two], axis=0)
    far_remote = far_lists.reshape(peer_count, far_count)
    far_owners = far_remote // node_count
    far_ranks = slot_ranks(far_owners)
    far_wanted = wanted_entries(far_owners, far_ranks, far_remote, device_index, far_slots)
    far_buffer = select(skeleton, far_wanted % node_count)
    far_arrived = lax.all_to_all(
        far_buffer.reshape(peer_count, far_slots, R, RANK),
        "leaf",
        split_axis=0,
        concat_axis=0,
        tiled=True,
    )
    my_far = lax.dynamic_index_in_dim(
        far_owners, device_index, 0, keepdims=False
    ) * far_slots + lax.dynamic_index_in_dim(far_ranks, device_index, 0, keepdims=False)
    partners = select(far_arrived.reshape(peer_count * far_slots, R, RANK), my_far).reshape(
        node_count, FAR, R, RANK
    )
    leaf_buffer = select(blocks, wanted % local_leaves)
    leaf_arrived = lax.all_to_all(
        leaf_buffer.reshape(peer_count, near_slots, FEAT + R, LEAF),
        "leaf",
        split_axis=0,
        concat_axis=0,
        tiled=True,
    )
    sources = select(leaf_arrived.reshape(peer_count * near_slots, FEAT + R, LEAF), my_slots)
    per_item = grouped_products(sources, jnp.repeat(points, NB - 1, axis=0))
    self_terms = tile_products(blocks, points)
    near = self_terms + jnp.sum(per_item.reshape(local_leaves, NB - 1, R, LEAF), axis=1)
    far = jnp.einsum("nfrk,nfkj->nrj", partners, far_blocks, preferred_element_type=jnp.float32)
    far_zero = far[:local_leaves]
    far_one = far[local_leaves : local_leaves * 3 // 2]
    far_two = far[local_leaves * 3 // 2 :]
    middle = descend(far_two, transfer_two, far_one)
    lowest = descend(middle, transfer_one, far_zero)
    result = near + jnp.einsum(
        "lrk,lak->lra", lowest.astype(jnp.bfloat16), basis, preferred_element_type=jnp.float32
    )
    return result.transpose(1, 0, 2).reshape(R, local_leaves * LEAF)


AUG = 16
CHUNK = 2
UNROLL = 4


def half_square_terms(points):
    points_f = points.astype(jnp.float32)
    half = -0.5 * jnp.sum(points_f * points_f, axis=0, keepdims=True)
    high = half.astype(jnp.bfloat16).astype(jnp.float32)
    rest = half - high
    middle = rest.astype(jnp.bfloat16).astype(jnp.float32)
    return high, middle, rest - middle


def extra_rows(points, first):
    shape = (AUG, points.shape[1])
    line = lax.broadcasted_iota(jnp.int32, shape, 0)
    ones = jnp.logical_and(line >= 3 - first, line < 6 - first)
    rows = jnp.where(ones, 1.0, 0.0)
    for at, term in enumerate(half_square_terms(points)):
        rows = jnp.where(line == first + at, jnp.broadcast_to(term, shape), rows)
    return rows.astype(jnp.bfloat16)


def tile(source, target, charge):
    exponent = lax.dot_general(
        source, target, (((0,), (0,)), ((), ())), preferred_element_type=jnp.float32
    )
    return jnp.dot(charge, jnp.exp(exponent).astype(jnp.bfloat16), preferred_element_type=jnp.float32)


def target_orders(rows):
    def key(at):
        return lambda row: (abs(row - at), abs(2 * row - rows + 1))

    return [sorted((row for row in range(rows) if row != at), key=key(at)) for at in range(rows)]


def whole_kernel(
    rows, parts, near, ends, far, coords_hbm, rhs_hbm, basis_hbm, one_hbm, two_hbm, blocks_hbm, out,
    own_points, across_points, points, own_charges, across_charges, edge_charges, cross_out, cross_in, skel, given, far_across,
    sums_out, sums_in, sources, targets, charges, skel_work, terms, far_out, far_at,
    basis, one, two, blocks,
    load_sem, leaf_sem, point_send, point_recv, peer_send, peer_recv, skel_send, skel_recv,
    sum_send, sum_recv, cross_send, cross_recv, given_send, given_recv, direct_send, direct_recv,
):
    leaves, nodes = basis.shape[0], skel.shape[1]
    share = FEAT // parts
    chunks = leaves // CHUNK
    leaf, part = lax.axis_index("leaf"), lax.axis_index("rhs")
    row, side = leaf // 2, leaf % 2
    across = (row * 2 + 1 - side, part)
    core_twin, y_twin = part + 1 - 2 * (part % 2), (part + 2) % parts
    mesh_ids = pl.DeviceIdType.MESH
    orders = target_orders(rows)

    def by_row(values):
        total = 0
        for at, value in enumerate(values):
            off = (row - at + rows) % rows
            total = total + value * (1 - (off + rows - 1) // rows)
        return total

    far_targets = [by_row([orders[at][k] for at in range(rows)]) for k in range(rows - 1)]
    ways = [by_row([int(orders[at][k] < at) for at in range(rows)]) for k in range(rows - 1)]

    loads = [
        pltpu.make_async_copy(source, target, load_sem.at[which])
        for which, (source, target) in enumerate(
            ((basis_hbm, basis), (one_hbm, one), (two_hbm, two), (blocks_hbm, blocks))
        )
    ]
    leaf_loads = [
        pltpu.make_async_copy(
            source.at[:, pl.ds(index * LEAF, LEAF)], target.at[index], leaf_sem.at[which, index]
        )
        for which, (source, target) in enumerate(
            ((coords_hbm, own_points), (rhs_hbm, own_charges))
        )
        for index in range(leaves)
    ]
    for load in leaf_loads + loads:
        load.start()

    barrier = pltpu.get_barrier_semaphore()
    partners = [across] + [(leaf, twin) for twin in (core_twin, y_twin)]
    for partner in partners:
        pl.semaphore_signal(barrier, inc=1, device_id=partner, device_id_type=mesh_ids)

    @pl.when(row > 0)
    def _():
        pl.semaphore_signal(barrier, inc=1, device_id=(leaf - 2, part), device_id_type=mesh_ids)

    @pl.when(row < rows - 1)
    def _():
        pl.semaphore_signal(barrier, inc=1, device_id=(leaf + 2, part), device_id_type=mesh_ids)

    ahead = (row + rows - 1) // rows + (2 * rows - 2 - row) // rows
    pl.semaphore_wait(barrier, len(partners) + ahead)

    def remote(source, target, send, recv, device):
        return pltpu.make_async_remote_copy(
            src_ref=source, dst_ref=target, send_sem=send, recv_sem=recv,
            device_id=device, device_id_type=mesh_ids,
        )

    def neighbour(way):
        return (leaf + 2 - 4 * way, part)

    my_share = pl.ds(pl.multiple_of(part * share, share), share)

    def point_hop(origin, way, own=False):
        source = own_points.at[:, my_share, :] if own else points.at[origin, :, my_share, :]
        return remote(
            source, points.at[origin, :, my_share, :], point_send.at[origin, way],
            point_recv.at[origin], neighbour(way),
        )

    half = leaves // 2
    skel_parts = (pl.ds(0, half), pl.ds(half, leaves - half), pl.ds(leaves, nodes - leaves))

    def skel_hop(origin, way, piece):
        held = skel.at[origin, skel_parts[piece]]
        return remote(
            held, held, skel_send.at[origin, piece, way], skel_recv.at[origin, piece],
            neighbour(way),
        )

    def cross(which):
        if which == 0:
            source, target = own_points.at[:, my_share, :], across_points.at[:, my_share, :]
        elif which == 1:
            source, target = own_charges, across_charges
        else:
            source, target = cross_out, cross_in
        return remote(source, target, cross_send.at[which], cross_recv.at[which], across)

    inward = row * 2 // rows

    def direct():
        return remote(
            own_charges, edge_charges, direct_send.at[0], direct_recv.at[0], neighbour(inward)
        )

    def given_hop(origin):
        return remote(
            given.at[origin], far_across.at[origin], given_send.at[origin],
            given_recv.at[origin], across,
        )

    y_share = pl.ds(pl.multiple_of(y_twin * share, share), share)

    def to_peer(unit, step):
        span = y_share if step == 2 else my_share
        if unit is None:
            held, at = across_points.at[:, span, :], rows
        else:
            held, at = points.at[unit, :, span, :], unit
        device = (leaf, y_twin if step == 0 else core_twin)
        return remote(held, held, peer_send.at[at, step], peer_recv.at[at, step], device)

    def share_points(unit):
        to_peer(unit, 0).start()
        to_peer(unit, 1).start()

    def pass_points(unit):
        to_peer(unit, 0).wait_recv()
        to_peer(unit, 2).start()

    def shared(unit):
        to_peer(unit, 1).wait_recv()
        to_peer(unit, 2).wait_recv()

    def sum_hop(target, way, chunk):
        span = pl.ds(chunk * CHUNK, CHUNK)
        return remote(
            sums_out.at[target, span], sums_in.at[way, target, span], sum_send.at[target, chunk],
            sum_recv.at[way, target, chunk], neighbour(way),
        )

    def flow(distance, arrive, onward):
        @pl.when(row >= distance)
        def _():
            origin = row - distance
            if distance:
                arrive(origin)

            @pl.when(row < rows - 1)
            def _():
                onward(origin, 0)

        @pl.when(row + distance < rows)
        def _():
            origin = row + distance
            if distance:
                arrive(origin)

            @pl.when(row > 0)
            def _():
                onward(origin, 1)

    def at_distance(distance, action):
        pl.when(row >= distance)(lambda: action(row - distance))
        pl.when(row + distance < rows)(lambda: action(row + distance))

    def relay_points(distance):
        flow(
            distance,
            lambda origin: point_hop(origin, 0).wait_recv(),
            lambda origin, way: point_hop(origin, way, distance == 0).start(),
        )

    def relay_skel(distance, piece):
        flow(
            distance,
            lambda origin: skel_hop(origin, 0, piece).wait_recv(),
            lambda origin, way: skel_hop(origin, way, piece).start(),
        )

    def fill(unit, from_points):
        for index in range(leaves):
            taken = from_points(index)
            targets[unit * leaves + index, :FEAT] = taken
            targets[unit * leaves + index, FEAT:] = extra_rows(taken, 3)

    def fill_sources(first, from_points, from_charges):
        for index in range(leaves):
            taken = from_points[index]
            sources[first + index, :FEAT] = taken
            sources[first + index, FEAT:] = extra_rows(taken, 0)
            charges[first + index] = from_charges[index]

    def run_tiles(place):
        def entry(index, carry):
            at = place * leaves + index
            source = near[0, at]
            term = tile(sources[source], targets[near[1, at]], charges[source])
            kept = jnp.where(near[2, at] == 1, 0.0, terms[at])
            terms[at + 1] = kept + term
            return carry

        lax.fori_loop(0, leaves, entry, 0, unroll=UNROLL)

    def near_sum(target, index):
        at = target * leaves + index
        return terms[ends[at]] + terms[ends[rows * leaves + at]]

    def edge_sums(k):
        target, way = far_targets[k], ways[k]

        def send():
            for chunk in range(chunks):
                for index in range(chunk * CHUNK, (chunk + 1) * CHUNK):
                    sums_out[target, index] = near_sum(target, index).astype(jnp.bfloat16)
                sum_hop(target, way, chunk).start()

        pl.when(jnp.logical_or(row == 0, row == rows - 1))(send)

    def inner_sums(k, chunk):
        target, way = far_targets[k], ways[k]

        def send():
            sum_hop(target, way, chunk).wait_recv()
            for index in range(chunk * CHUNK, (chunk + 1) * CHUNK):
                arrived = sums_in[way, target, index].astype(jnp.float32)
                sums_out[target, index] = (near_sum(target, index) + arrived).astype(jnp.bfloat16)
            sum_hop(target, way, chunk).start()

        pl.when(jnp.logical_and(row > 0, row < rows - 1))(send)

    def far_product(weights, at):
        far_out[at] = jnp.dot(weights, blocks[far[1, at]], preferred_element_type=jnp.float32)

    def give(origin):
        skel_work[...] = skel[origin]
        for index in range(leaves):
            given[origin, index] = skel_work[far[3, origin * leaves + index]]
        given_hop(origin).start()

    def far_own(origin):
        skel_work[...] = skel[origin]

        def entry(index, carry):
            at = origin * leaves + index
            far_product(skel_work[far[0, at]], at)
            return carry

        lax.fori_loop(0, leaves, entry, 0, unroll=UNROLL)

    def far_beside(origin):
        given_hop(origin).wait_recv()

        def entry(index, carry):
            far_product(far_across[origin, index], (rows + origin) * leaves + index)
            return carry

        lax.fori_loop(0, leaves, entry, 0, unroll=UNROLL)

    for load in leaf_loads:
        load.wait()
    relay_points(0)
    cross(0).start()
    cross(1).start()
    terms[0] = jnp.zeros_like(terms[0])
    fill_sources(0, own_points, own_charges)
    fill(row, lambda index: own_points[index])

    for load in loads[:3]:
        load.wait()
    first_one, first_two = leaves, leaves * 3 // 2

    def joined(first, transfer):
        left = jnp.dot(skel[row, first], transfer[:RANK], preferred_element_type=jnp.float32)
        right = jnp.dot(skel[row, first + 1], transfer[RANK:], preferred_element_type=jnp.float32)
        return (left + right).astype(jnp.bfloat16)

    def leaf_skel(index):
        skel[row, index] = jnp.dot(
            own_charges[index], basis[index], preferred_element_type=jnp.float32
        ).astype(jnp.bfloat16)

    def at_edge(action):
        pl.when(jnp.logical_or(row == 0, row == rows - 1))(action)

    def inside(action):
        pl.when(jnp.logical_and(row > 0, row < rows - 1))(action)

    first, second, third = far_targets

    for index in range(half):
        leaf_skel(index)
    relay_skel(0, 0)
    for index in range(half, leaves):
        leaf_skel(index)
    for index in range(first_two - first_one):
        skel[row, first_one + index] = joined(2 * index, one[index])
    for index in range(nodes - first_two):
        skel[row, first_two + index] = joined(first_one + 2 * index, two[index])
    relay_points(1)
    share_points(first)
    cross(0).wait_recv()
    share_points(None)
    inside(lambda: share_points(second))
    relay_skel(0, 1)
    relay_skel(0, 2)
    at_edge(lambda: direct().start())
    give(row)
    run_tiles(row)
    pass_points(first)
    relay_points(2)
    at_edge(lambda: share_points(second))
    inside(lambda: share_points(third))
    shared(first)

    def first_tiles():
        fill(first, lambda index: points[first, index])
        run_tiles(first)

    inside(first_tiles)
    relay_skel(1, 0)
    pass_points(None)
    pass_points(second)
    relay_points(3)
    at_edge(lambda: share_points(third))
    shared(second)
    fill(second, lambda index: points[second, index])
    run_tiles(second)
    relay_skel(1, 1)
    relay_skel(1, 2)
    at_distance(1, give)
    shared(None)
    cross(1).wait_recv()
    fill_sources(leaves, across_points, across_charges)
    inside(lambda: run_tiles(rows + first))
    run_tiles(rows + second)
    edge_sums(1)
    pass_points(third)
    shared(third)
    fill(third, lambda index: points[third, index])
    run_tiles(third)
    inner_sums(0, 0)
    run_tiles(rows + third)
    edge_sums(2)
    inner_sums(0, 1)
    inner_sums(0, 2)
    for piece in range(3):
        relay_skel(2, piece)
    at_distance(2, give)
    edge = row * 2 // rows * (rows - 1)

    def direct_tiles():
        direct().wait_recv()
        fill_sources(2 * leaves, points.at[edge], edge_charges)
        fill(rows, lambda index: across_points[index])
        run_tiles(2 * rows + 1)
        for index in range(leaves):
            cross_out[index] = terms[ends[(2 * rows + 1) * leaves + index]].astype(jnp.bfloat16)
        cross(2).start()

    inside(direct_tiles)
    inner_sums(0, 3)
    run_tiles(rows + row)
    inner_sums(2, 0)
    inside(lambda: run_tiles(2 * rows))
    loads[3].wait()
    inner_sums(2, 1)
    inner_sums(1, 0)
    at_distance(1, far_own)
    far_beside(row)
    inner_sums(2, 2)
    inner_sums(1, 1)
    at_distance(1, far_beside)
    inner_sums(2, 3)
    inner_sums(1, 2)
    at_distance(2, far_own)
    inner_sums(1, 3)
    for piece in range(3):
        relay_skel(3, piece)
    at_distance(3, give)
    at_distance(2, far_beside)
    at_distance(3, far_own)
    at_distance(3, far_beside)

    for node in range(nodes):
        total = far_out[far[2, node * FAR]]
        for partner in range(1, FAR):
            total = total + far_out[far[2, node * FAR + partner]]
        far_at[node] = total

    def spread_to(parent, transfer):
        return lax.dot_general(
            parent.astype(jnp.bfloat16), transfer, (((1,), (1,)), ((), ())),
            preferred_element_type=jnp.float32,
        )

    for parent in range(nodes - first_two):
        spread = spread_to(far_at[first_two + parent], two[parent])
        for child in range(2):
            far_at[first_one + 2 * parent + child] += spread[:, child * RANK : (child + 1) * RANK]
    for parent in range(first_two - first_one):
        spread = spread_to(far_at[first_one + parent], one[parent])
        for child in range(2):
            far_at[2 * parent + child] += spread[:, child * RANK : (child + 1) * RANK]
    for index in range(leaves):
        out[:, index * LEAF : (index + 1) * LEAF] = near_sum(row, index) + spread_to(
            far_at[index], basis[index]
        )

    def add_arrived(way, chunk):
        sum_hop(row, way, chunk).wait_recv()
        for index in range(chunk * CHUNK, (chunk + 1) * CHUNK):
            span = slice(index * LEAF, (index + 1) * LEAF)
            out[:, span] += sums_in[way, row, index].astype(jnp.float32)

    def add_cross():
        cross(2).wait_recv()
        for index in range(leaves):
            span = slice(index * LEAF, (index + 1) * LEAF)
            direct_sum = terms[ends[2 * rows * leaves + index]]
            out[:, span] += direct_sum + cross_in[index].astype(jnp.float32)

    inside(add_cross)
    for chunk in range(chunks):
        pl.when(2 * row >= rows)(functools.partial(add_arrived, 0, chunk))
        pl.when(2 * row < rows)(functools.partial(add_arrived, 1, chunk))

    for distance in range(rows):
        flow(
            distance,
            lambda origin: None,
            lambda origin, way: point_hop(origin, way, distance == 0).wait_send(),
        )
        for piece in range(3):
            flow(
                distance,
                lambda origin: None,
                lambda origin, way: skel_hop(origin, way, piece).wait_send(),
            )
    for which in range(2):
        cross(which).wait_send()
    for origin in range(rows):
        given_hop(origin).wait_send()
    for step in range(3):
        to_peer(None, step).wait_send()
        for k in range(rows - 1):
            to_peer(far_targets[k], step).wait_send()
    at_edge(lambda: direct().wait_send())
    inside(lambda: cross(2).wait_send())
    for chunk in range(chunks):
        inside(lambda: sum_hop(first, ways[0], chunk).wait_send())
        for k in range(1, rows - 1):
            sum_hop(far_targets[k], ways[k], chunk).wait_send()


def on_device(coords, rhs, basis, transfer_one, transfer_two, far_blocks, neighbours, far_lists):
    peer_count = lax.axis_size("leaf")
    whole_lists = peer_count == NB and peer_count % 2 == 0
    even_lists = far_blocks.shape[0] * FAR == (NB - 1) * basis.shape[0]
    even_shares = lax.axis_size("rhs") == 4 and FEAT % lax.axis_size("rhs") == 0
    route = gathered if whole_lists and even_lists and even_shares else exchanged
    return route(coords, rhs, basis, transfer_one, transfer_two, far_blocks, neighbours, far_lists)


def chosen_entries(matches, ranks, values, count):
    slots = jnp.arange(count, dtype=jnp.int32)
    taken = matches[..., None, :] & (ranks[..., None, :] == slots[:, None])
    return jnp.sum(jnp.where(taken, values[..., None, :], 0), axis=-1)


def route_tables(rows, leaves, nodes, row, side, neighbours, far_lists):
    listed = leaves * NB
    by_place = neighbours.reshape(rows, 2, listed)
    column = lax.dynamic_index_in_dim(by_place, side, 1, keepdims=False)
    pair = lax.dynamic_index_in_dim(by_place, row, 0, keepdims=False)
    couple = jnp.where(side == 0, pair, pair[::-1])
    lists = jnp.concatenate([column, column, couple])
    place = jnp.arange(2 * rows + 2, dtype=jnp.int32)
    group = place // rows
    edge = row * 2 // rows * (rows - 1)
    own = jnp.where(group == 2, edge, row) * 2 + jnp.where(group == 1, 1 - side, side)
    unit = jnp.where(group < 2, place % rows, jnp.where(place == 2 * rows, row, rows))
    matches = lists // leaves == own[:, None]
    position = jnp.arange(listed, dtype=jnp.int32)
    earlier = position[None, :] < position[:, None]
    same_leaf = position[None, :] // NB == position[:, None] // NB
    counted = matches[:, None, :]
    ranks = jnp.sum(counted & earlier, axis=2, dtype=jnp.int32)
    opens = jnp.sum(counted & earlier & same_leaf, axis=2, dtype=jnp.int32) == 0
    source = group[:, None] * leaves + lists % leaves
    target = unit[:, None] * leaves + position // NB
    wide = (rows + 1) * leaves
    values = (source * wide + target) * 2 + opens
    picked = chosen_entries(matches, ranks, values, leaves).reshape(-1)
    near = jnp.stack([picked // (2 * wide), picked // 2 % wide, picked % 2])
    leaf_of = position // NB
    leaf_ids = jnp.arange(leaves, dtype=jnp.int32)[:, None]
    upto = jnp.sum(counted & (leaf_of <= leaf_ids), axis=2, dtype=jnp.int32)
    some = jnp.any(counted & (leaf_of == leaf_ids), axis=2)
    ends = jnp.where(some, place[:, None] * leaves + upto, 0).reshape(-1)

    count = nodes * FAR
    peers = far_lists.reshape(rows, 2, count)
    pair = lax.dynamic_index_in_dim(peers, row, 0, keepdims=False)
    mine = lax.dynamic_index_in_dim(pair, side, 0, keepdims=False)
    beside = lax.dynamic_index_in_dim(pair, 1 - side, 0, keepdims=False)
    lists = jnp.stack([mine, beside])
    sides = jnp.stack([side, 1 - side])[:, None]
    owners = lists // nodes
    slot = (owners + sides) % 2 * rows + owners // 2
    entry = jnp.arange(count, dtype=jnp.int32)
    before = entry[None, :] < entry[:, None]
    rank = jnp.sum((slot[:, :, None] == slot[:, None, :]) & before, axis=2, dtype=jnp.int32)
    at = slot * leaves + rank
    wide = 2 * rows * leaves
    chosen = chosen_entries(jnp.full((2, count), True), at, lists % nodes * count + entry, wide)
    far = jnp.stack(
        [
            chosen[0] // count,
            chosen[0] % count,
            jnp.pad(at[0], (0, wide - count)),
            jnp.roll(chosen[1] // count, -rows * leaves),
        ]
    )
    return near, ends, far


def gathered(coords, rhs, basis, transfer_one, transfer_two, far_blocks, neighbours, far_lists):
    peer_count = lax.axis_size("leaf")
    parts = lax.axis_size("rhs")
    rows = peer_count // 2
    device_index = lax.axis_index("leaf")
    leaves, nodes = basis.shape[0], far_blocks.shape[0]
    tables = route_tables(
        rows, leaves, nodes, device_index // 2, device_index % 2, neighbours, far_lists
    )
    smem = pl.BlockSpec(memory_space=pltpu.SMEM)
    anywhere = pl.BlockSpec(memory_space=pl.ANY)
    bf16, f32 = jnp.bfloat16, jnp.float32
    chunks = leaves // CHUNK
    dma = pltpu.SemaphoreType.DMA
    return pl.pallas_call(
        functools.partial(whole_kernel, rows, parts),
        out_shape=jax.ShapeDtypeStruct((R, rhs.shape[1]), f32),
        in_specs=[smem] * 3 + [anywhere] * 6,
        out_specs=pl.BlockSpec(memory_space=pltpu.VMEM),
        scratch_shapes=[
            pltpu.VMEM((leaves, FEAT, LEAF), bf16),
            pltpu.VMEM((leaves, FEAT, LEAF), bf16),
            pltpu.VMEM((rows, leaves, FEAT, LEAF), bf16),
            pltpu.VMEM((leaves, R, LEAF), bf16),
            pltpu.VMEM((leaves, R, LEAF), bf16),
            pltpu.VMEM((leaves, R, LEAF), bf16),
            pltpu.VMEM((leaves, R, LEAF), bf16),
            pltpu.VMEM((leaves, R, LEAF), bf16),
            pltpu.VMEM((rows, nodes, R, RANK), bf16),
            pltpu.VMEM((rows, leaves, R, RANK), bf16),
            pltpu.VMEM((rows, leaves, R, RANK), bf16),
            pltpu.VMEM((rows, leaves, R, LEAF), bf16),
            pltpu.VMEM((2, rows, leaves, R, LEAF), bf16),
            pltpu.VMEM((3 * leaves, FEAT + AUG, LEAF), bf16),
            pltpu.VMEM(((rows + 1) * leaves, FEAT + AUG, LEAF), bf16),
            pltpu.VMEM((3 * leaves, R, LEAF), bf16),
            pltpu.VMEM((nodes, R, RANK), bf16),
            pltpu.VMEM(((peer_count + 2) * leaves + 1, R, LEAF), f32),
            pltpu.VMEM((peer_count * leaves, R, RANK), f32),
            pltpu.VMEM((nodes, R, RANK), f32),
            pltpu.VMEM(basis.shape, bf16),
            pltpu.VMEM(transfer_one.shape, bf16),
            pltpu.VMEM(transfer_two.shape, bf16),
            pltpu.VMEM((nodes * FAR, RANK, RANK), bf16),
            dma((4,)),
            dma((2, leaves)),
            dma((rows, 2)),
            dma((rows,)),
            dma((rows + 1, 3)),
            dma((rows + 1, 3)),
            dma((rows, 3, 2)),
            dma((rows, 3)),
            dma((rows, chunks)),
            dma((2, rows, chunks)),
            dma((3,)),
            dma((3,)),
            dma((rows,)),
            dma((rows,)),
            dma((1,)),
            dma((1,)),
        ],
        compiler_params=pltpu.CompilerParams(
            collective_id=0, has_side_effects=True, vmem_limit_bytes=60 * 1024 * 1024
        ),
        name="whole",
    )(
        *tables, coords, rhs, basis, transfer_one, transfer_two,
        far_blocks.reshape(nodes * FAR, RANK, RANK),
    )


def solution(mesh):
    return jax.shard_map(
        on_device,
        mesh=mesh,
        in_specs=(
            P(None, "leaf"),
            P("rhs", "leaf"),
            P("leaf", None, None),
            P("leaf", None, None),
            P("leaf", None, None),
            P("leaf", None, None, None),
            P(),
            P(),
        ),
        out_specs=P("rhs", "leaf"),
        check_vma=False,
    )
```

```python
import functools

import jax
import jax.numpy as jnp
from jax import lax
from jax.experimental import pallas as pl
from jax.experimental.pallas import tpu as pltpu
from jax.sharding import PartitionSpec as P

FEAT = 64
RANK = 256
R = 64
LEAF = 512
NB = 8
FAR = 4


def kernel_tiles(sources, targets):
    inner = jnp.einsum("...fa,...fb->...ab", sources, targets, preferred_element_type=jnp.float32)
    src_f = sources.astype(jnp.float32)
    dst_f = targets.astype(jnp.float32)
    src_sq = jnp.sum(src_f * src_f, axis=-2)
    dst_sq = jnp.sum(dst_f * dst_f, axis=-2)
    return jnp.exp(inner - 0.5 * src_sq[..., :, None] - 0.5 * dst_sq[..., None, :]).astype(
        jnp.bfloat16
    )


def tile_products(sources, targets):
    kernel = kernel_tiles(sources[:, :FEAT], targets)
    return jnp.einsum("gra,gab->grb", sources[:, FEAT:], kernel, preferred_element_type=jnp.float32)


def grouped_products(sources, targets):
    groups = sources.shape[0] // 4
    paired = (
        sources.reshape(groups, 4, sources.shape[1], sources.shape[2]),
        targets.reshape(groups, 4, targets.shape[1], targets.shape[2]),
    )
    outcome = lax.map(lambda couple: tile_products(couple[0], couple[1]), paired)
    return outcome.reshape(sources.shape[0], R, sources.shape[2])


def slot_ranks(owners):
    entry_count = owners.shape[1]
    position = jnp.arange(entry_count, dtype=jnp.int32)
    earlier = position[None, :] < position[:, None]
    matches = owners[:, :, None] == owners[:, None, :]
    return jnp.sum(jnp.logical_and(matches, earlier[None]), axis=2)


def wanted_entries(owners, ranks, entries, device_index, slot_count):
    slots = jnp.arange(slot_count, dtype=jnp.int32)
    taken = (owners == device_index)[:, None, :] & (ranks[:, None, :] == slots[:, None])
    return jnp.sum(jnp.where(taken, entries[:, None, :], 0), axis=2).reshape(-1)


def select(items, indices):
    taken = (indices[:, None] == jnp.arange(items.shape[0], dtype=jnp.int32)).astype(items.dtype)
    return jnp.einsum("sn,nrk->srk", taken, items, preferred_element_type=jnp.float32).astype(items.dtype)


def join_pairs(skeleton):
    return skeleton.reshape(-1, 2, R, RANK).transpose(0, 2, 1, 3).reshape(-1, R, 2 * RANK)


def descend(parent, transfer, child_far):
    rounded = parent.astype(jnp.bfloat16)
    spread = jnp.einsum("mrk,mjk->mrj", rounded, transfer, preferred_element_type=jnp.float32)
    spread = spread.reshape(-1, R, 2, RANK).transpose(0, 2, 1, 3).reshape(-1, R, RANK)
    return child_far + spread


def exchanged(coords, rhs, basis, transfer_one, transfer_two, far_blocks, neighbours, far_lists):
    peer_count = lax.axis_size("leaf")
    device_index = lax.axis_index("leaf")
    local_leaves = basis.shape[0]
    node_count = far_blocks.shape[0]
    remote_count = (NB - 1) * local_leaves
    near_slots = (remote_count + peer_count - 2) // (peer_count - 1)
    far_count = node_count * FAR
    far_slots = (far_count + peer_count - 2) // (peer_count - 1)
    points = coords.reshape(FEAT, local_leaves, LEAF).transpose(1, 0, 2)
    charges = rhs.reshape(R, local_leaves, LEAF).transpose(1, 0, 2)
    blocks = jnp.concatenate([points, charges], axis=1)
    remote = neighbours.reshape(peer_count, local_leaves, NB)[:, :, 1:].reshape(
        peer_count, remote_count
    )
    owners = remote // local_leaves
    ranks = slot_ranks(owners)
    my_owners = lax.dynamic_index_in_dim(owners, device_index, 0, keepdims=False)
    my_ranks = lax.dynamic_index_in_dim(ranks, device_index, 0, keepdims=False)
    my_slots = my_owners * near_slots + my_ranks
    wanted = wanted_entries(owners, ranks, remote, device_index, near_slots)
    skel_zero = jnp.einsum(
        "lra,lak->lrk", charges, basis, preferred_element_type=jnp.float32
    ).astype(jnp.bfloat16)
    skel_one = jnp.einsum(
        "mrj,mjk->mrk", join_pairs(skel_zero), transfer_one, preferred_element_type=jnp.float32
    ).astype(jnp.bfloat16)
    skel_two = jnp.einsum(
        "mrj,mjk->mrk", join_pairs(skel_one), transfer_two, preferred_element_type=jnp.float32
    ).astype(jnp.bfloat16)
    skeleton = jnp.concatenate([skel_zero, skel_one, skel_two], axis=0)
    far_remote = far_lists.reshape(peer_count, far_count)
    far_owners = far_remote // node_count
    far_ranks = slot_ranks(far_owners)
    far_wanted = wanted_entries(far_owners, far_ranks, far_remote, device_index, far_slots)
    far_buffer = select(skeleton, far_wanted % node_count)
    far_arrived = lax.all_to_all(
        far_buffer.reshape(peer_count, far_slots, R, RANK),
        "leaf",
        split_axis=0,
        concat_axis=0,
        tiled=True,
    )
    my_far = lax.dynamic_index_in_dim(
        far_owners, device_index, 0, keepdims=False
    ) * far_slots + lax.dynamic_index_in_dim(far_ranks, device_index, 0, keepdims=False)
    partners = select(far_arrived.reshape(peer_count * far_slots, R, RANK), my_far).reshape(
        node_count, FAR, R, RANK
    )
    leaf_buffer = select(blocks, wanted % local_leaves)
    leaf_arrived = lax.all_to_all(
        leaf_buffer.reshape(peer_count, near_slots, FEAT + R, LEAF),
        "leaf",
        split_axis=0,
        concat_axis=0,
        tiled=True,
    )
    sources = select(leaf_arrived.reshape(peer_count * near_slots, FEAT + R, LEAF), my_slots)
    per_item = grouped_products(sources, jnp.repeat(points, NB - 1, axis=0))
    self_terms = tile_products(blocks, points)
    near = self_terms + jnp.sum(per_item.reshape(local_leaves, NB - 1, R, LEAF), axis=1)
    far = jnp.einsum("nfrk,nfkj->nrj", partners, far_blocks, preferred_element_type=jnp.float32)
    far_zero = far[:local_leaves]
    far_one = far[local_leaves : local_leaves * 3 // 2]
    far_two = far[local_leaves * 3 // 2 :]
    middle = descend(far_two, transfer_two, far_one)
    lowest = descend(middle, transfer_one, far_zero)
    result = near + jnp.einsum(
        "lrk,lak->lra", lowest.astype(jnp.bfloat16), basis, preferred_element_type=jnp.float32
    )
    return result.transpose(1, 0, 2).reshape(R, local_leaves * LEAF)


AUG = 16
CHUNK = 2
UNROLL = 8


def half_square_terms(points):
    points_f = points.astype(jnp.float32)
    half = -0.5 * jnp.sum(points_f * points_f, axis=0, keepdims=True)
    high = half.astype(jnp.bfloat16).astype(jnp.float32)
    rest = half - high
    middle = rest.astype(jnp.bfloat16).astype(jnp.float32)
    return high, middle, rest - middle


def extra_rows(points, first):
    shape = (AUG, points.shape[1])
    line = lax.broadcasted_iota(jnp.int32, shape, 0)
    ones = jnp.logical_and(line >= 3 - first, line < 6 - first)
    rows = jnp.where(ones, 1.0, 0.0)
    for at, term in enumerate(half_square_terms(points)):
        rows = jnp.where(line == first + at, jnp.broadcast_to(term, shape), rows)
    return rows.astype(jnp.bfloat16)


def tile(source, target, charge):
    exponent = lax.dot_general(
        source, target, (((0,), (0,)), ((), ())), preferred_element_type=jnp.float32
    )
    return jnp.dot(charge, jnp.exp(exponent).astype(jnp.bfloat16), preferred_element_type=jnp.float32)


def target_orders(rows):
    def key(at):
        return lambda row: (abs(row - at), abs(2 * row - rows + 1))

    return [sorted((row for row in range(rows) if row != at), key=key(at)) for at in range(rows)]


def whole_kernel(
    rows, parts, near, coords_hbm, rhs_hbm, basis_hbm, one_hbm, two_hbm, blocks_hbm, out,
    own_points, across_points, points, own_charges, across_charges, edge_charges, cross_out, cross_in, skel, given, far_across,
    sums_out, sums_in, sources, targets, charges, skel_work, terms, far_out, far_at,
    basis, one, two, blocks,
    load_sem, leaf_sem, point_send, point_recv, peer_send, peer_recv, skel_send, skel_recv,
    sum_send, sum_recv, cross_send, cross_recv, given_send, given_recv, direct_send, direct_recv,
):
    leaves, nodes = basis.shape[0], skel.shape[1]
    share = FEAT // parts
    chunks = leaves // CHUNK
    leaf, part = lax.axis_index("leaf"), lax.axis_index("rhs")
    row, side = leaf // 2, leaf % 2
    across = (row * 2 + 1 - side, part)
    core_twin, y_twin = part + 1 - 2 * (part % 2), (part + 2) % parts
    mesh_ids = pl.DeviceIdType.MESH
    orders = target_orders(rows)

    def by_row(values):
        total = 0
        for at, value in enumerate(values):
            off = (row - at + rows) % rows
            total = total + value * (1 - (off + rows - 1) // rows)
        return total

    far_targets = [by_row([orders[at][k] for at in range(rows)]) for k in range(rows - 1)]
    ways = [by_row([int(orders[at][k] < at) for at in range(rows)]) for k in range(rows - 1)]

    loads = [
        pltpu.make_async_copy(source, target, load_sem.at[which])
        for which, (source, target) in enumerate(
            ((basis_hbm, basis), (one_hbm, one), (two_hbm, two), (blocks_hbm, blocks))
        )
    ]
    leaf_loads = [
        pltpu.make_async_copy(
            source.at[:, pl.ds(index * LEAF, LEAF)], target.at[index], leaf_sem.at[which, index]
        )
        for which, (source, target) in enumerate(
            ((coords_hbm, own_points), (rhs_hbm, own_charges))
        )
        for index in range(leaves)
    ]
    for load in leaf_loads + loads:
        load.start()

    barrier = pltpu.get_barrier_semaphore()
    partners = [across] + [(leaf, twin) for twin in (core_twin, y_twin)]
    for partner in partners:
        pl.semaphore_signal(barrier, inc=1, device_id=partner, device_id_type=mesh_ids)

    @pl.when(row > 0)
    def _():
        pl.semaphore_signal(barrier, inc=1, device_id=(leaf - 2, part), device_id_type=mesh_ids)

    @pl.when(row < rows - 1)
    def _():
        pl.semaphore_signal(barrier, inc=1, device_id=(leaf + 2, part), device_id_type=mesh_ids)

    ahead = (row + rows - 1) // rows + (2 * rows - 2 - row) // rows
    pl.semaphore_wait(barrier, len(partners) + ahead)

    def remote(source, target, send, recv, device):
        return pltpu.make_async_remote_copy(
            src_ref=source, dst_ref=target, send_sem=send, recv_sem=recv,
            device_id=device, device_id_type=mesh_ids,
        )

    def neighbour(way):
        return (leaf + 2 - 4 * way, part)

    my_share = pl.ds(pl.multiple_of(part * share, share), share)

    def point_hop(origin, way, own=False):
        source = own_points.at[:, my_share, :] if own else points.at[origin, :, my_share, :]
        return remote(
            source, points.at[origin, :, my_share, :], point_send.at[origin, way],
            point_recv.at[origin], neighbour(way),
        )

    half = leaves // 2
    skel_parts = (pl.ds(0, half), pl.ds(half, leaves - half), pl.ds(leaves, nodes - leaves))

    def skel_hop(origin, way, piece):
        held = skel.at[origin, skel_parts[piece]]
        return remote(
            held, held, skel_send.at[origin, piece, way], skel_recv.at[origin, piece],
            neighbour(way),
        )

    def cross(which):
        if which == 0:
            source, target = own_points.at[:, my_share, :], across_points.at[:, my_share, :]
        elif which == 1:
            source, target = own_charges, across_charges
        else:
            source, target = cross_out, cross_in
        return remote(source, target, cross_send.at[which], cross_recv.at[which], across)

    inward = row * 2 // rows

    def direct():
        return remote(
            own_charges, edge_charges, direct_send.at[0], direct_recv.at[0], neighbour(inward)
        )

    def given_hop(origin):
        return remote(
            given.at[origin], far_across.at[origin], given_send.at[origin],
            given_recv.at[origin], across,
        )

    y_share = pl.ds(pl.multiple_of(y_twin * share, share), share)

    def to_peer(unit, step):
        span = y_share if step == 2 else my_share
        if unit is None:
            held, at = across_points.at[:, span, :], rows
        else:
            held, at = points.at[unit, :, span, :], unit
        device = (leaf, y_twin if step == 0 else core_twin)
        return remote(held, held, peer_send.at[at, step], peer_recv.at[at, step], device)

    def share_points(unit):
        to_peer(unit, 0).start()
        to_peer(unit, 1).start()

    def pass_points(unit):
        to_peer(unit, 0).wait_recv()
        to_peer(unit, 2).start()

    def shared(unit):
        to_peer(unit, 1).wait_recv()
        to_peer(unit, 2).wait_recv()

    def sum_hop(target, way, chunk):
        span = pl.ds(chunk * CHUNK, CHUNK)
        return remote(
            sums_out.at[target, span], sums_in.at[way, target, span], sum_send.at[target, chunk],
            sum_recv.at[way, target, chunk], neighbour(way),
        )

    def flow(distance, arrive, onward):
        @pl.when(row >= distance)
        def _():
            origin = row - distance
            if distance:
                arrive(origin)

            @pl.when(row < rows - 1)
            def _():
                onward(origin, 0)

        @pl.when(row + distance < rows)
        def _():
            origin = row + distance
            if distance:
                arrive(origin)

            @pl.when(row > 0)
            def _():
                onward(origin, 1)

    def at_distance(distance, action):
        pl.when(row >= distance)(lambda: action(row - distance))
        pl.when(row + distance < rows)(lambda: action(row + distance))

    def relay_points(distance):
        flow(
            distance,
            lambda origin: point_hop(origin, 0).wait_recv(),
            lambda origin, way: point_hop(origin, way, distance == 0).start(),
        )

    def relay_skel(distance, piece):
        flow(
            distance,
            lambda origin: skel_hop(origin, 0, piece).wait_recv(),
            lambda origin, way: skel_hop(origin, way, piece).start(),
        )

    def fill(unit, from_points):
        for index in range(leaves):
            taken = from_points(index)
            targets[unit * leaves + index, :FEAT] = taken
            targets[unit * leaves + index, FEAT:] = extra_rows(taken, 3)

    def fill_sources(first, from_points, from_charges):
        for index in range(leaves):
            taken = from_points[index]
            sources[first + index, :FEAT] = taken
            sources[first + index, FEAT:] = extra_rows(taken, 0)
            charges[first + index] = from_charges[index]

    def run_tiles(place):
        def entry(index, carry):
            at = place * leaves + index
            source = near[0, at]
            term = tile(sources[source], targets[near[1, at]], charges[source])
            kept = jnp.where(near[2, at] == 1, 0.0, terms[at])
            terms[at + 1] = kept + term
            return carry

        lax.fori_loop(0, leaves, entry, 0, unroll=UNROLL)

    def near_sum(target, index):
        at = target * leaves + index
        return terms[near[3, at]] + terms[near[3, rows * leaves + at]]

    def edge_sums(k):
        target, way = far_targets[k], ways[k]

        def send():
            for chunk in range(chunks):
                for index in range(chunk * CHUNK, (chunk + 1) * CHUNK):
                    sums_out[target, index] = near_sum(target, index).astype(jnp.bfloat16)
                sum_hop(target, way, chunk).start()

        pl.when(jnp.logical_or(row == 0, row == rows - 1))(send)

    def inner_sums(k, chunk):
        target, way = far_targets[k], ways[k]

        def send():
            sum_hop(target, way, chunk).wait_recv()
            for index in range(chunk * CHUNK, (chunk + 1) * CHUNK):
                arrived = sums_in[way, target, index].astype(jnp.float32)
                sums_out[target, index] = (near_sum(target, index) + arrived).astype(jnp.bfloat16)
            sum_hop(target, way, chunk).start()

        pl.when(jnp.logical_and(row > 0, row < rows - 1))(send)

    def far_product(weights, at):
        far_out[at] = jnp.dot(weights, blocks[near[5, at]], preferred_element_type=jnp.float32)

    def give(origin):
        skel_work[...] = skel[origin]
        for index in range(leaves):
            given[origin, index] = skel_work[near[7, origin * leaves + index]]
        given_hop(origin).start()

    def far_own(origin):
        skel_work[...] = skel[origin]

        def entry(index, carry):
            at = origin * leaves + index
            far_product(skel_work[near[4, at]], at)
            return carry

        lax.fori_loop(0, leaves, entry, 0, unroll=UNROLL)

    def far_beside(origin):
        given_hop(origin).wait_recv()

        def entry(index, carry):
            far_product(far_across[origin, index], (rows + origin) * leaves + index)
            return carry

        lax.fori_loop(0, leaves, entry, 0, unroll=UNROLL)

    for load in leaf_loads[:leaves]:
        load.wait()
    relay_points(0)
    cross(0).start()
    for load in leaf_loads[leaves:]:
        load.wait()
    cross(1).start()
    terms[0] = jnp.zeros_like(terms[0])
    fill_sources(0, own_points, own_charges)
    fill(row, lambda index: own_points[index])

    for load in loads[:3]:
        load.wait()
    first_one, first_two = leaves, leaves * 3 // 2

    def joined(first, transfer):
        left = jnp.dot(skel[row, first], transfer[:RANK], preferred_element_type=jnp.float32)
        right = jnp.dot(skel[row, first + 1], transfer[RANK:], preferred_element_type=jnp.float32)
        return (left + right).astype(jnp.bfloat16)

    def leaf_skel(index):
        skel[row, index] = jnp.dot(
            own_charges[index], basis[index], preferred_element_type=jnp.float32
        ).astype(jnp.bfloat16)

    def at_edge(action):
        pl.when(jnp.logical_or(row == 0, row == rows - 1))(action)

    def inside(action):
        pl.when(jnp.logical_and(row > 0, row < rows - 1))(action)

    first, second, third = far_targets

    for index in range(half):
        leaf_skel(index)
    for index in range(half, leaves):
        leaf_skel(index)
    for index in range(first_two - first_one):
        skel[row, first_one + index] = joined(2 * index, one[index])
    for index in range(nodes - first_two):
        skel[row, first_two + index] = joined(first_one + 2 * index, two[index])
    relay_points(1)
    share_points(first)
    cross(0).wait_recv()
    share_points(None)
    inside(lambda: share_points(second))
    relay_skel(0, 0)
    relay_skel(0, 1)
    relay_skel(0, 2)
    at_edge(lambda: direct().start())
    give(row)
    run_tiles(row)
    pass_points(first)
    relay_points(2)
    at_edge(lambda: share_points(second))
    inside(lambda: share_points(third))
    shared(first)

    def first_tiles():
        fill(first, lambda index: points[first, index])
        run_tiles(first)

    relay_skel(1, 0)
    inside(first_tiles)
    pass_points(None)
    pass_points(second)
    relay_points(3)
    at_edge(lambda: share_points(third))
    shared(second)
    fill(second, lambda index: points[second, index])
    relay_skel(1, 1)
    run_tiles(second)
    relay_skel(1, 2)
    at_distance(1, give)
    shared(None)
    cross(1).wait_recv()
    fill_sources(leaves, across_points, across_charges)
    inside(lambda: run_tiles(rows + first))
    relay_skel(2, 0)
    run_tiles(rows + second)
    edge_sums(1)
    pass_points(third)
    shared(third)
    fill(third, lambda index: points[third, index])
    run_tiles(third)
    relay_skel(2, 1)
    inner_sums(0, 0)
    relay_skel(2, 2)
    run_tiles(rows + third)
    edge_sums(2)
    inner_sums(0, 1)
    inner_sums(0, 2)
    at_distance(2, give)
    edge = row * 2 // rows * (rows - 1)

    def direct_tiles():
        direct().wait_recv()
        fill_sources(2 * leaves, points.at[edge], edge_charges)
        fill(rows, lambda index: across_points[index])
        run_tiles(2 * rows + 1)
        for index in range(leaves):
            cross_out[index] = terms[near[3, (2 * rows + 1) * leaves + index]].astype(jnp.bfloat16)
        cross(2).start()

    inside(direct_tiles)
    inner_sums(0, 3)
    run_tiles(rows + row)
    inner_sums(2, 0)
    inside(lambda: run_tiles(2 * rows))
    loads[3].wait()
    inner_sums(2, 1)
    inner_sums(1, 0)
    at_distance(1, far_own)
    far_beside(row)
    inner_sums(2, 2)
    inner_sums(1, 1)
    at_distance(1, far_beside)
    inner_sums(2, 3)
    inner_sums(1, 2)
    at_distance(2, far_own)
    inner_sums(1, 3)
    for piece in range(3):
        relay_skel(3, piece)
    at_distance(3, give)
    at_distance(2, far_beside)
    at_distance(3, far_own)
    at_distance(3, far_beside)

    for node in range(nodes):
        total = far_out[near[6, node * FAR]]
        for partner in range(1, FAR):
            total = total + far_out[near[6, node * FAR + partner]]
        far_at[node] = total

    def spread_to(parent, transfer):
        return lax.dot_general(
            parent.astype(jnp.bfloat16), transfer, (((1,), (1,)), ((), ())),
            preferred_element_type=jnp.float32,
        )

    for parent in range(nodes - first_two):
        spread = spread_to(far_at[first_two + parent], two[parent])
        for child in range(2):
            far_at[first_one + 2 * parent + child] += spread[:, child * RANK : (child + 1) * RANK]
    for parent in range(first_two - first_one):
        spread = spread_to(far_at[first_one + parent], one[parent])
        for child in range(2):
            far_at[2 * parent + child] += spread[:, child * RANK : (child + 1) * RANK]
    for index in range(leaves):
        out[:, index * LEAF : (index + 1) * LEAF] = near_sum(row, index) + spread_to(
            far_at[index], basis[index]
        )

    def add_arrived(way, chunk):
        sum_hop(row, way, chunk).wait_recv()
        for index in range(chunk * CHUNK, (chunk + 1) * CHUNK):
            span = slice(index * LEAF, (index + 1) * LEAF)
            out[:, span] += sums_in[way, row, index].astype(jnp.float32)

    def add_cross():
        cross(2).wait_recv()
        for index in range(leaves):
            span = slice(index * LEAF, (index + 1) * LEAF)
            direct_sum = terms[near[3, 2 * rows * leaves + index]]
            out[:, span] += direct_sum + cross_in[index].astype(jnp.float32)

    inside(add_cross)
    for chunk in range(chunks):
        pl.when(2 * row >= rows)(functools.partial(add_arrived, 0, chunk))
        pl.when(2 * row < rows)(functools.partial(add_arrived, 1, chunk))

    for distance in range(rows):
        flow(
            distance,
            lambda origin: None,
            lambda origin, way: point_hop(origin, way, distance == 0).wait_send(),
        )
        for piece in range(3):
            flow(
                distance,
                lambda origin: None,
                lambda origin, way: skel_hop(origin, way, piece).wait_send(),
            )
    for which in range(2):
        cross(which).wait_send()
    for origin in range(rows):
        given_hop(origin).wait_send()
    for step in range(3):
        to_peer(None, step).wait_send()
        for k in range(rows - 1):
            to_peer(far_targets[k], step).wait_send()
    at_edge(lambda: direct().wait_send())
    inside(lambda: cross(2).wait_send())
    for chunk in range(chunks):
        inside(lambda: sum_hop(first, ways[0], chunk).wait_send())
        for k in range(1, rows - 1):
            sum_hop(far_targets[k], ways[k], chunk).wait_send()


def on_device(coords, rhs, basis, transfer_one, transfer_two, far_blocks, neighbours, far_lists):
    peer_count = lax.axis_size("leaf")
    whole_lists = peer_count == NB and peer_count % 2 == 0
    even_lists = far_blocks.shape[0] * FAR == (NB - 1) * basis.shape[0]
    even_shares = lax.axis_size("rhs") == 4 and FEAT % lax.axis_size("rhs") == 0
    route = gathered if whole_lists and even_lists and even_shares else exchanged
    return route(coords, rhs, basis, transfer_one, transfer_two, far_blocks, neighbours, far_lists)


def chosen_entries(matches, ranks, values, count):
    slots = jnp.arange(count, dtype=jnp.int32)
    taken = matches[..., None, :] & (ranks[..., None, :] == slots[:, None])
    return jnp.sum(jnp.where(taken, values[..., None, :], 0), axis=-1)


def route_tables(rows, leaves, nodes, row, side, neighbours, far_lists):
    listed = leaves * NB
    by_place = neighbours.reshape(rows, 2, listed)
    column = lax.dynamic_index_in_dim(by_place, side, 1, keepdims=False)
    pair = lax.dynamic_index_in_dim(by_place, row, 0, keepdims=False)
    couple = jnp.where(side == 0, pair, pair[::-1])
    lists = jnp.concatenate([column, column, couple])
    place = jnp.arange(2 * rows + 2, dtype=jnp.int32)
    group = place // rows
    edge = row * 2 // rows * (rows - 1)
    own = jnp.where(group == 2, edge, row) * 2 + jnp.where(group == 1, 1 - side, side)
    unit = jnp.where(group < 2, place % rows, jnp.where(place == 2 * rows, row, rows))
    matches = lists // leaves == own[:, None]
    position = jnp.arange(listed, dtype=jnp.int32)
    earlier = position[None, :] < position[:, None]
    same_leaf = position[None, :] // NB == position[:, None] // NB
    counted = matches[:, None, :]
    ranks = jnp.sum(counted & earlier, axis=2, dtype=jnp.int32)
    opens = jnp.sum(counted & earlier & same_leaf, axis=2, dtype=jnp.int32) == 0
    source = group[:, None] * leaves + lists % leaves
    target = unit[:, None] * leaves + position // NB
    wide = (rows + 1) * leaves
    values = (source * wide + target) * 2 + opens
    picked = chosen_entries(matches, ranks, values, leaves).reshape(-1)
    near = [picked // (2 * wide), picked // 2 % wide, picked % 2]
    leaf_of = position // NB
    leaf_ids = jnp.arange(leaves, dtype=jnp.int32)[:, None]
    upto = jnp.sum(counted & (leaf_of <= leaf_ids), axis=2, dtype=jnp.int32)
    some = jnp.any(counted & (leaf_of == leaf_ids), axis=2)
    ends = jnp.where(some, place[:, None] * leaves + upto, 0).reshape(-1)

    count = nodes * FAR
    peers = far_lists.reshape(rows, 2, count)
    pair = lax.dynamic_index_in_dim(peers, row, 0, keepdims=False)
    mine = lax.dynamic_index_in_dim(pair, side, 0, keepdims=False)
    beside = lax.dynamic_index_in_dim(pair, 1 - side, 0, keepdims=False)
    lists = jnp.stack([mine, beside])
    sides = jnp.stack([side, 1 - side])[:, None]
    owners = lists // nodes
    slot = (owners + sides) % 2 * rows + owners // 2
    entry = jnp.arange(count, dtype=jnp.int32)
    before = entry[None, :] < entry[:, None]
    rank = jnp.sum((slot[:, :, None] == slot[:, None, :]) & before, axis=2, dtype=jnp.int32)
    at = slot * leaves + rank
    wide = 2 * rows * leaves
    chosen = chosen_entries(jnp.full((2, count), True), at, lists % nodes * count + entry, wide)
    beside_picks = chosen[1, rows * leaves :] // count
    lines = near + [ends, chosen[0] // count, chosen[0] % count, at[0], beside_picks]
    longest = max(line.shape[0] for line in lines)
    return jnp.stack([jnp.pad(line, (0, longest - line.shape[0])) for line in lines])


def gathered(coords, rhs, basis, transfer_one, transfer_two, far_blocks, neighbours, far_lists):
    peer_count = lax.axis_size("leaf")
    parts = lax.axis_size("rhs")
    rows = peer_count // 2
    device_index = lax.axis_index("leaf")
    leaves, nodes = basis.shape[0], far_blocks.shape[0]
    table = route_tables(
        rows, leaves, nodes, device_index // 2, device_index % 2, neighbours, far_lists
    )
    smem = pl.BlockSpec(memory_space=pltpu.SMEM)
    anywhere = pl.BlockSpec(memory_space=pl.ANY)
    bf16, f32 = jnp.bfloat16, jnp.float32
    chunks = leaves // CHUNK
    dma = pltpu.SemaphoreType.DMA
    return pl.pallas_call(
        functools.partial(whole_kernel, rows, parts),
        out_shape=jax.ShapeDtypeStruct((R, rhs.shape[1]), f32),
        in_specs=[smem] + [anywhere] * 6,
        out_specs=pl.BlockSpec(memory_space=pltpu.VMEM),
        scratch_shapes=[
            pltpu.VMEM((leaves, FEAT, LEAF), bf16),
            pltpu.VMEM((leaves, FEAT, LEAF), bf16),
            pltpu.VMEM((rows, leaves, FEAT, LEAF), bf16),
            pltpu.VMEM((leaves, R, LEAF), bf16),
            pltpu.VMEM((leaves, R, LEAF), bf16),
            pltpu.VMEM((leaves, R, LEAF), bf16),
            pltpu.VMEM((leaves, R, LEAF), bf16),
            pltpu.VMEM((leaves, R, LEAF), bf16),
            pltpu.VMEM((rows, nodes, R, RANK), bf16),
            pltpu.VMEM((rows, leaves, R, RANK), bf16),
            pltpu.VMEM((rows, leaves, R, RANK), bf16),
            pltpu.VMEM((rows, leaves, R, LEAF), bf16),
            pltpu.VMEM((2, rows, leaves, R, LEAF), bf16),
            pltpu.VMEM((3 * leaves, FEAT + AUG, LEAF), bf16),
            pltpu.VMEM(((rows + 1) * leaves, FEAT + AUG, LEAF), bf16),
            pltpu.VMEM((3 * leaves, R, LEAF), bf16),
            pltpu.VMEM((nodes, R, RANK), bf16),
            pltpu.VMEM(((peer_count + 2) * leaves + 1, R, LEAF), f32),
            pltpu.VMEM((peer_count * leaves, R, RANK), f32),
            pltpu.VMEM((nodes, R, RANK), f32),
            pltpu.VMEM(basis.shape, bf16),
            pltpu.VMEM(transfer_one.shape, bf16),
            pltpu.VMEM(transfer_two.shape, bf16),
            pltpu.VMEM((nodes * FAR, RANK, RANK), bf16),
            dma((4,)),
            dma((2, leaves)),
            dma((rows, 2)),
            dma((rows,)),
            dma((rows + 1, 3)),
            dma((rows + 1, 3)),
            dma((rows, 3, 2)),
            dma((rows, 3)),
            dma((rows, chunks)),
            dma((2, rows, chunks)),
            dma((3,)),
            dma((3,)),
            dma((rows,)),
            dma((rows,)),
            dma((1,)),
            dma((1,)),
        ],
        compiler_params=pltpu.CompilerParams(
            collective_id=0, has_side_effects=True, vmem_limit_bytes=60 * 1024 * 1024
        ),
        name="whole",
    )(
        table, coords, rhs, basis, transfer_one, transfer_two,
        far_blocks.reshape(nodes * FAR, RANK, RANK),
    )


def solution(mesh):
    return jax.shard_map(
        on_device,
        mesh=mesh,
        in_specs=(
            P(None, "leaf"),
            P("rhs", "leaf"),
            P("leaf", None, None),
            P("leaf", None, None),
            P("leaf", None, None),
            P("leaf", None, None, None),
            P(),
            P(),
        ),
        out_specs=P("rhs", "leaf"),
        check_vma=False,
    )
```

```python
import functools

import jax
import jax.numpy as jnp
from jax import lax
from jax.experimental import pallas as pl
from jax.experimental.pallas import tpu as pltpu
from jax.sharding import PartitionSpec as P

FEAT = 64
RANK = 256
R = 64
LEAF = 512
NB = 8
FAR = 4


def kernel_tiles(sources, targets):
    inner = jnp.einsum("...fa,...fb->...ab", sources, targets, preferred_element_type=jnp.float32)
    src_f = sources.astype(jnp.float32)
    dst_f = targets.astype(jnp.float32)
    src_sq = jnp.sum(src_f * src_f, axis=-2)
    dst_sq = jnp.sum(dst_f * dst_f, axis=-2)
    return jnp.exp(inner - 0.5 * src_sq[..., :, None] - 0.5 * dst_sq[..., None, :]).astype(
        jnp.bfloat16
    )


def tile_products(sources, targets):
    kernel = kernel_tiles(sources[:, :FEAT], targets)
    return jnp.einsum("gra,gab->grb", sources[:, FEAT:], kernel, preferred_element_type=jnp.float32)


def grouped_products(sources, targets):
    groups = sources.shape[0] // 4
    paired = (
        sources.reshape(groups, 4, sources.shape[1], sources.shape[2]),
        targets.reshape(groups, 4, targets.shape[1], targets.shape[2]),
    )
    outcome = lax.map(lambda couple: tile_products(couple[0], couple[1]), paired)
    return outcome.reshape(sources.shape[0], R, sources.shape[2])


def slot_ranks(owners):
    entry_count = owners.shape[1]
    position = jnp.arange(entry_count, dtype=jnp.int32)
    earlier = position[None, :] < position[:, None]
    matches = owners[:, :, None] == owners[:, None, :]
    return jnp.sum(jnp.logical_and(matches, earlier[None]), axis=2)


def wanted_entries(owners, ranks, entries, device_index, slot_count):
    slots = jnp.arange(slot_count, dtype=jnp.int32)
    taken = (owners == device_index)[:, None, :] & (ranks[:, None, :] == slots[:, None])
    return jnp.sum(jnp.where(taken, entries[:, None, :], 0), axis=2).reshape(-1)


def select(items, indices):
    taken = (indices[:, None] == jnp.arange(items.shape[0], dtype=jnp.int32)).astype(items.dtype)
    return jnp.einsum("sn,nrk->srk", taken, items, preferred_element_type=jnp.float32).astype(items.dtype)


def join_pairs(skeleton):
    return skeleton.reshape(-1, 2, R, RANK).transpose(0, 2, 1, 3).reshape(-1, R, 2 * RANK)


def descend(parent, transfer, child_far):
    rounded = parent.astype(jnp.bfloat16)
    spread = jnp.einsum("mrk,mjk->mrj", rounded, transfer, preferred_element_type=jnp.float32)
    spread = spread.reshape(-1, R, 2, RANK).transpose(0, 2, 1, 3).reshape(-1, R, RANK)
    return child_far + spread


def exchanged(coords, rhs, basis, transfer_one, transfer_two, far_blocks, neighbours, far_lists):
    peer_count = lax.axis_size("leaf")
    device_index = lax.axis_index("leaf")
    local_leaves = basis.shape[0]
    node_count = far_blocks.shape[0]
    remote_count = (NB - 1) * local_leaves
    near_slots = (remote_count + peer_count - 2) // (peer_count - 1)
    far_count = node_count * FAR
    far_slots = (far_count + peer_count - 2) // (peer_count - 1)
    points = coords.reshape(FEAT, local_leaves, LEAF).transpose(1, 0, 2)
    charges = rhs.reshape(R, local_leaves, LEAF).transpose(1, 0, 2)
    blocks = jnp.concatenate([points, charges], axis=1)
    remote = neighbours.reshape(peer_count, local_leaves, NB)[:, :, 1:].reshape(
        peer_count, remote_count
    )
    owners = remote // local_leaves
    ranks = slot_ranks(owners)
    my_owners = lax.dynamic_index_in_dim(owners, device_index, 0, keepdims=False)
    my_ranks = lax.dynamic_index_in_dim(ranks, device_index, 0, keepdims=False)
    my_slots = my_owners * near_slots + my_ranks
    wanted = wanted_entries(owners, ranks, remote, device_index, near_slots)
    skel_zero = jnp.einsum(
        "lra,lak->lrk", charges, basis, preferred_element_type=jnp.float32
    ).astype(jnp.bfloat16)
    skel_one = jnp.einsum(
        "mrj,mjk->mrk", join_pairs(skel_zero), transfer_one, preferred_element_type=jnp.float32
    ).astype(jnp.bfloat16)
    skel_two = jnp.einsum(
        "mrj,mjk->mrk", join_pairs(skel_one), transfer_two, preferred_element_type=jnp.float32
    ).astype(jnp.bfloat16)
    skeleton = jnp.concatenate([skel_zero, skel_one, skel_two], axis=0)
    far_remote = far_lists.reshape(peer_count, far_count)
    far_owners = far_remote // node_count
    far_ranks = slot_ranks(far_owners)
    far_wanted = wanted_entries(far_owners, far_ranks, far_remote, device_index, far_slots)
    far_buffer = select(skeleton, far_wanted % node_count)
    far_arrived = lax.all_to_all(
        far_buffer.reshape(peer_count, far_slots, R, RANK),
        "leaf",
        split_axis=0,
        concat_axis=0,
        tiled=True,
    )
    my_far = lax.dynamic_index_in_dim(
        far_owners, device_index, 0, keepdims=False
    ) * far_slots + lax.dynamic_index_in_dim(far_ranks, device_index, 0, keepdims=False)
    partners = select(far_arrived.reshape(peer_count * far_slots, R, RANK), my_far).reshape(
        node_count, FAR, R, RANK
    )
    leaf_buffer = select(blocks, wanted % local_leaves)
    leaf_arrived = lax.all_to_all(
        leaf_buffer.reshape(peer_count, near_slots, FEAT + R, LEAF),
        "leaf",
        split_axis=0,
        concat_axis=0,
        tiled=True,
    )
    sources = select(leaf_arrived.reshape(peer_count * near_slots, FEAT + R, LEAF), my_slots)
    per_item = grouped_products(sources, jnp.repeat(points, NB - 1, axis=0))
    self_terms = tile_products(blocks, points)
    near = self_terms + jnp.sum(per_item.reshape(local_leaves, NB - 1, R, LEAF), axis=1)
    far = jnp.einsum("nfrk,nfkj->nrj", partners, far_blocks, preferred_element_type=jnp.float32)
    far_zero = far[:local_leaves]
    far_one = far[local_leaves : local_leaves * 3 // 2]
    far_two = far[local_leaves * 3 // 2 :]
    middle = descend(far_two, transfer_two, far_one)
    lowest = descend(middle, transfer_one, far_zero)
    result = near + jnp.einsum(
        "lrk,lak->lra", lowest.astype(jnp.bfloat16), basis, preferred_element_type=jnp.float32
    )
    return result.transpose(1, 0, 2).reshape(R, local_leaves * LEAF)


AUG = 16
CHUNK = 1
UNROLL = 8


def half_square_terms(points):
    points_f = points.astype(jnp.float32)
    half = -0.5 * jnp.sum(points_f * points_f, axis=0, keepdims=True)
    high = half.astype(jnp.bfloat16).astype(jnp.float32)
    rest = half - high
    middle = rest.astype(jnp.bfloat16).astype(jnp.float32)
    return high, middle, rest - middle


def extra_rows(points, first):
    shape = (AUG, points.shape[1])
    line = lax.broadcasted_iota(jnp.int32, shape, 0)
    ones = jnp.logical_and(line >= 3 - first, line < 6 - first)
    rows = jnp.where(ones, 1.0, 0.0)
    for at, term in enumerate(half_square_terms(points)):
        rows = jnp.where(line == first + at, jnp.broadcast_to(term, shape), rows)
    return rows.astype(jnp.bfloat16)


def tile(source, target, charge):
    exponent = lax.dot_general(
        source, target, (((0,), (0,)), ((), ())), preferred_element_type=jnp.float32
    )
    return jnp.dot(charge, jnp.exp(exponent).astype(jnp.bfloat16), preferred_element_type=jnp.float32)


def target_orders(rows):
    def key(at):
        return lambda row: (abs(row - at), abs(2 * row - rows + 1))

    return [sorted((row for row in range(rows) if row != at), key=key(at)) for at in range(rows)]


def whole_kernel(
    rows, parts, near, coords_hbm, rhs_hbm, basis_hbm, one_hbm, two_hbm, blocks_hbm, out,
    own_points, across_points, points, own_charges, across_charges, edge_charges, cross_out, cross_in, skel, given, far_across,
    sums_out, sums_in, sources, targets, charges, skel_work, terms, far_out, far_at,
    basis, one, two, blocks,
    load_sem, leaf_sem, point_send, point_recv, peer_send, peer_recv, skel_send, skel_recv,
    sum_send, sum_recv, cross_send, cross_recv, given_send, given_recv, direct_send, direct_recv,
):
    leaves, nodes = basis.shape[0], skel.shape[1]
    share = FEAT // parts
    chunks = leaves // CHUNK
    leaf, part = lax.axis_index("leaf"), lax.axis_index("rhs")
    row, side = leaf // 2, leaf % 2
    across = (row * 2 + 1 - side, part)
    core_twin, y_twin = part + 1 - 2 * (part % 2), (part + 2) % parts
    mesh_ids = pl.DeviceIdType.MESH
    orders = target_orders(rows)

    def by_row(values):
        total = 0
        for at, value in enumerate(values):
            off = (row - at + rows) % rows
            total = total + value * (1 - (off + rows - 1) // rows)
        return total

    far_targets = [by_row([orders[at][k] for at in range(rows)]) for k in range(rows - 1)]
    ways = [by_row([int(orders[at][k] < at) for at in range(rows)]) for k in range(rows - 1)]

    loads = [
        pltpu.make_async_copy(source, target, load_sem.at[which])
        for which, (source, target) in enumerate(
            ((basis_hbm, basis), (one_hbm, one), (two_hbm, two), (blocks_hbm, blocks))
        )
    ]
    leaf_loads = [
        pltpu.make_async_copy(
            source.at[:, pl.ds(index * LEAF, LEAF)], target.at[index], leaf_sem.at[which, index]
        )
        for which, (source, target) in enumerate(
            ((coords_hbm, own_points), (rhs_hbm, own_charges))
        )
        for index in range(leaves)
    ]
    for load in leaf_loads + loads:
        load.start()

    barrier = pltpu.get_barrier_semaphore()
    partners = [across] + [(leaf, twin) for twin in (core_twin, y_twin)]
    for partner in partners:
        pl.semaphore_signal(barrier, inc=1, device_id=partner, device_id_type=mesh_ids)

    @pl.when(row > 0)
    def _():
        pl.semaphore_signal(barrier, inc=1, device_id=(leaf - 2, part), device_id_type=mesh_ids)

    @pl.when(row < rows - 1)
    def _():
        pl.semaphore_signal(barrier, inc=1, device_id=(leaf + 2, part), device_id_type=mesh_ids)

    ahead = (row + rows - 1) // rows + (2 * rows - 2 - row) // rows
    pl.semaphore_wait(barrier, len(partners) + ahead)

    def remote(source, target, send, recv, device):
        return pltpu.make_async_remote_copy(
            src_ref=source, dst_ref=target, send_sem=send, recv_sem=recv,
            device_id=device, device_id_type=mesh_ids,
        )

    def neighbour(way):
        return (leaf + 2 - 4 * way, part)

    my_share = pl.ds(pl.multiple_of(part * share, share), share)

    def point_hop(origin, way, own=False):
        source = own_points.at[:, my_share, :] if own else points.at[origin, :, my_share, :]
        return remote(
            source, points.at[origin, :, my_share, :], point_send.at[origin, way],
            point_recv.at[origin], neighbour(way),
        )

    half = leaves // 2
    skel_parts = (pl.ds(0, half), pl.ds(half, leaves - half), pl.ds(leaves, nodes - leaves))

    def skel_hop(origin, way, piece):
        held = skel.at[origin, skel_parts[piece]]
        return remote(
            held, held, skel_send.at[origin, piece, way], skel_recv.at[origin, piece],
            neighbour(way),
        )

    def cross(which):
        if which == 0:
            source, target = own_points.at[:, my_share, :], across_points.at[:, my_share, :]
        elif which == 1:
            source, target = own_charges, across_charges
        else:
            source, target = cross_out, cross_in
        return remote(source, target, cross_send.at[which], cross_recv.at[which], across)

    inward = row * 2 // rows

    def direct():
        return remote(
            own_charges, edge_charges, direct_send.at[0], direct_recv.at[0], neighbour(inward)
        )

    def given_hop(origin):
        return remote(
            given.at[origin], far_across.at[origin], given_send.at[origin],
            given_recv.at[origin], across,
        )

    y_share = pl.ds(pl.multiple_of(y_twin * share, share), share)

    def to_peer(unit, step):
        span = y_share if step == 2 else my_share
        if unit is None:
            held, at = across_points.at[:, span, :], rows
        else:
            held, at = points.at[unit, :, span, :], unit
        device = (leaf, y_twin if step == 0 else core_twin)
        return remote(held, held, peer_send.at[at, step], peer_recv.at[at, step], device)

    def share_points(unit):
        to_peer(unit, 0).start()
        to_peer(unit, 1).start()

    def pass_points(unit):
        to_peer(unit, 0).wait_recv()
        to_peer(unit, 2).start()

    def shared(unit):
        to_peer(unit, 1).wait_recv()
        to_peer(unit, 2).wait_recv()

    def sum_hop(target, way, chunk):
        span = pl.ds(chunk * CHUNK, CHUNK)
        return remote(
            sums_out.at[target, span], sums_in.at[way, target, span], sum_send.at[target, chunk],
            sum_recv.at[way, target, chunk], neighbour(way),
        )

    def flow(distance, arrive, onward):
        @pl.when(row >= distance)
        def _():
            origin = row - distance
            if distance:
                arrive(origin)

            @pl.when(row < rows - 1)
            def _():
                onward(origin, 0)

        @pl.when(row + distance < rows)
        def _():
            origin = row + distance
            if distance:
                arrive(origin)

            @pl.when(row > 0)
            def _():
                onward(origin, 1)

    def at_distance(distance, action):
        pl.when(row >= distance)(lambda: action(row - distance))
        pl.when(row + distance < rows)(lambda: action(row + distance))

    def relay_points(distance):
        flow(
            distance,
            lambda origin: point_hop(origin, 0).wait_recv(),
            lambda origin, way: point_hop(origin, way, distance == 0).start(),
        )

    def relay_skel(distance, piece):
        flow(
            distance,
            lambda origin: skel_hop(origin, 0, piece).wait_recv(),
            lambda origin, way: skel_hop(origin, way, piece).start(),
        )

    def fill(unit, from_points):
        for index in range(leaves):
            taken = from_points(index)
            targets[unit * leaves + index, :FEAT] = taken
            targets[unit * leaves + index, FEAT:] = extra_rows(taken, 3)

    def fill_sources(first, from_points, from_charges):
        for index in range(leaves):
            taken = from_points[index]
            sources[first + index, :FEAT] = taken
            sources[first + index, FEAT:] = extra_rows(taken, 0)
            charges[first + index] = from_charges[index]

    def run_tiles(place):
        def entry(index, carry):
            at = place * leaves + index
            source = near[0, at]
            term = tile(sources[source], targets[near[1, at]], charges[source])
            kept = jnp.where(near[2, at] == 1, 0.0, terms[at])
            terms[at + 1] = kept + term
            return carry

        lax.fori_loop(0, leaves, entry, 0, unroll=UNROLL)

    def near_sum(target, index):
        at = target * leaves + index
        return terms[near[3, at]] + terms[near[3, rows * leaves + at]]

    def edge_sums(k):
        target, way = far_targets[k], ways[k]

        def send():
            for chunk in range(chunks):
                for index in range(chunk * CHUNK, (chunk + 1) * CHUNK):
                    sums_out[target, index] = near_sum(target, index).astype(jnp.bfloat16)
                sum_hop(target, way, chunk).start()

        pl.when(jnp.logical_or(row == 0, row == rows - 1))(send)

    def inner_sums(k, quarter):
        target, way = far_targets[k], ways[k]

        def send():
            for chunk in range(quarter * chunks // 4, (quarter + 1) * chunks // 4):
                sum_hop(target, way, chunk).wait_recv()
                for index in range(chunk * CHUNK, (chunk + 1) * CHUNK):
                    arrived = sums_in[way, target, index].astype(jnp.float32)
                    total = near_sum(target, index) + arrived
                    sums_out[target, index] = total.astype(jnp.bfloat16)
                sum_hop(target, way, chunk).start()

        pl.when(jnp.logical_and(row > 0, row < rows - 1))(send)

    def far_product(weights, at):
        far_out[at] = jnp.dot(weights, blocks[near[5, at]], preferred_element_type=jnp.float32)

    def give(origin):
        skel_work[...] = skel[origin]
        for index in range(leaves):
            given[origin, index] = skel_work[near[7, origin * leaves + index]]
        given_hop(origin).start()

    def far_own(origin):
        skel_work[...] = skel[origin]

        def entry(index, carry):
            at = origin * leaves + index
            far_product(skel_work[near[4, at]], at)
            return carry

        lax.fori_loop(0, leaves, entry, 0, unroll=UNROLL)

    def far_beside(origin):
        given_hop(origin).wait_recv()

        def entry(index, carry):
            far_product(far_across[origin, index], (rows + origin) * leaves + index)
            return carry

        lax.fori_loop(0, leaves, entry, 0, unroll=UNROLL)

    for load in leaf_loads[:leaves]:
        load.wait()
    relay_points(0)
    cross(0).start()
    for load in leaf_loads[leaves:]:
        load.wait()
    cross(1).start()
    terms[0] = jnp.zeros_like(terms[0])
    fill_sources(0, own_points, own_charges)
    fill(row, lambda index: own_points[index])

    for load in loads[:3]:
        load.wait()
    first_one, first_two = leaves, leaves * 3 // 2

    def joined(first, transfer):
        left = jnp.dot(skel[row, first], transfer[:RANK], preferred_element_type=jnp.float32)
        right = jnp.dot(skel[row, first + 1], transfer[RANK:], preferred_element_type=jnp.float32)
        return (left + right).astype(jnp.bfloat16)

    def leaf_skel(index):
        skel[row, index] = jnp.dot(
            own_charges[index], basis[index], preferred_element_type=jnp.float32
        ).astype(jnp.bfloat16)

    def at_edge(action):
        pl.when(jnp.logical_or(row == 0, row == rows - 1))(action)

    def inside(action):
        pl.when(jnp.logical_and(row > 0, row < rows - 1))(action)

    first, second, third = far_targets

    for index in range(half):
        leaf_skel(index)
    for index in range(half, leaves):
        leaf_skel(index)
    for index in range(first_two - first_one):
        skel[row, first_one + index] = joined(2 * index, one[index])
    for index in range(nodes - first_two):
        skel[row, first_two + index] = joined(first_one + 2 * index, two[index])
    relay_points(1)
    share_points(first)
    cross(0).wait_recv()
    share_points(None)
    inside(lambda: share_points(second))
    relay_skel(0, 0)
    relay_skel(0, 1)
    relay_skel(0, 2)
    at_edge(lambda: direct().start())
    give(row)
    run_tiles(row)
    pass_points(first)
    relay_points(2)
    at_edge(lambda: share_points(second))
    inside(lambda: share_points(third))
    shared(first)

    def first_tiles():
        fill(first, lambda index: points[first, index])
        run_tiles(first)

    relay_skel(1, 0)
    inside(first_tiles)
    pass_points(None)
    pass_points(second)
    relay_points(3)
    at_edge(lambda: share_points(third))
    shared(second)
    fill(second, lambda index: points[second, index])
    relay_skel(1, 1)
    run_tiles(second)
    relay_skel(1, 2)
    at_distance(1, give)
    shared(None)
    cross(1).wait_recv()
    fill_sources(leaves, across_points, across_charges)
    inside(lambda: run_tiles(rows + first))
    relay_skel(2, 0)
    run_tiles(rows + second)
    edge_sums(1)
    pass_points(third)
    shared(third)
    fill(third, lambda index: points[third, index])
    run_tiles(third)
    relay_skel(2, 1)
    inner_sums(0, 0)
    relay_skel(2, 2)
    run_tiles(rows + third)
    edge_sums(2)
    inner_sums(0, 1)
    inner_sums(0, 2)
    at_distance(2, give)
    edge = row * 2 // rows * (rows - 1)

    def direct_tiles():
        direct().wait_recv()
        fill_sources(2 * leaves, points.at[edge], edge_charges)
        fill(rows, lambda index: across_points[index])
        run_tiles(2 * rows + 1)
        for index in range(leaves):
            cross_out[index] = terms[near[3, (2 * rows + 1) * leaves + index]].astype(jnp.bfloat16)
        cross(2).start()

    inside(direct_tiles)
    inner_sums(0, 3)
    run_tiles(rows + row)
    inner_sums(2, 0)
    inside(lambda: run_tiles(2 * rows))
    loads[3].wait()
    at_distance(1, far_own)
    far_beside(row)
    inner_sums(2, 1)
    inner_sums(1, 0)
    for piece in range(3):
        relay_skel(3, piece)
    at_distance(3, give)
    at_distance(1, far_beside)
    inner_sums(2, 2)
    inner_sums(1, 1)
    at_distance(2, far_own)
    at_distance(2, far_beside)
    at_distance(3, far_own)
    at_distance(3, far_beside)

    for node in range(nodes):
        total = far_out[near[6, node * FAR]]
        for partner in range(1, FAR):
            total = total + far_out[near[6, node * FAR + partner]]
        far_at[node] = total

    def spread_to(parent, transfer):
        return lax.dot_general(
            parent.astype(jnp.bfloat16), transfer, (((1,), (1,)), ((), ())),
            preferred_element_type=jnp.float32,
        )

    for parent in range(nodes - first_two):
        spread = spread_to(far_at[first_two + parent], two[parent])
        for child in range(2):
            far_at[first_one + 2 * parent + child] += spread[:, child * RANK : (child + 1) * RANK]
    for parent in range(first_two - first_one):
        spread = spread_to(far_at[first_one + parent], one[parent])
        for child in range(2):
            far_at[2 * parent + child] += spread[:, child * RANK : (child + 1) * RANK]
    inner_sums(2, 3)
    inner_sums(1, 2)
    for index in range(leaves):
        out[:, index * LEAF : (index + 1) * LEAF] = near_sum(row, index) + spread_to(
            far_at[index], basis[index]
        )

    inner_sums(1, 3)

    def add_arrived(way, chunk):
        sum_hop(row, way, chunk).wait_recv()
        for index in range(chunk * CHUNK, (chunk + 1) * CHUNK):
            span = slice(index * LEAF, (index + 1) * LEAF)
            out[:, span] += sums_in[way, row, index].astype(jnp.float32)

    def add_cross():
        cross(2).wait_recv()
        for index in range(leaves):
            span = slice(index * LEAF, (index + 1) * LEAF)
            direct_sum = terms[near[3, 2 * rows * leaves + index]]
            out[:, span] += direct_sum + cross_in[index].astype(jnp.float32)

    inside(add_cross)
    for chunk in range(chunks):
        pl.when(2 * row >= rows)(functools.partial(add_arrived, 0, chunk))
        pl.when(2 * row < rows)(functools.partial(add_arrived, 1, chunk))

    for distance in range(rows):
        flow(
            distance,
            lambda origin: None,
            lambda origin, way: point_hop(origin, way, distance == 0).wait_send(),
        )
        for piece in range(3):
            flow(
                distance,
                lambda origin: None,
                lambda origin, way: skel_hop(origin, way, piece).wait_send(),
            )
    for which in range(2):
        cross(which).wait_send()
    for origin in range(rows):
        given_hop(origin).wait_send()
    for step in range(3):
        to_peer(None, step).wait_send()
        for k in range(rows - 1):
            to_peer(far_targets[k], step).wait_send()
    at_edge(lambda: direct().wait_send())
    inside(lambda: cross(2).wait_send())
    for chunk in range(chunks):
        inside(lambda: sum_hop(first, ways[0], chunk).wait_send())
        for k in range(1, rows - 1):
            sum_hop(far_targets[k], ways[k], chunk).wait_send()


def on_device(coords, rhs, basis, transfer_one, transfer_two, far_blocks, neighbours, far_lists):
    peer_count = lax.axis_size("leaf")
    whole_lists = peer_count == NB and peer_count % 2 == 0
    even_lists = far_blocks.shape[0] * FAR == (NB - 1) * basis.shape[0]
    even_shares = lax.axis_size("rhs") == 4 and FEAT % lax.axis_size("rhs") == 0
    route = gathered if whole_lists and even_lists and even_shares else exchanged
    return route(coords, rhs, basis, transfer_one, transfer_two, far_blocks, neighbours, far_lists)


def chosen_entries(matches, ranks, values, count):
    slots = jnp.arange(count, dtype=jnp.int32)
    taken = matches[..., None, :] & (ranks[..., None, :] == slots[:, None])
    return jnp.sum(jnp.where(taken, values[..., None, :], 0), axis=-1)


def route_tables(rows, leaves, nodes, row, side, neighbours, far_lists):
    listed = leaves * NB
    by_place = neighbours.reshape(rows, 2, listed)
    column = lax.dynamic_index_in_dim(by_place, side, 1, keepdims=False)
    pair = lax.dynamic_index_in_dim(by_place, row, 0, keepdims=False)
    couple = jnp.where(side == 0, pair, pair[::-1])
    lists = jnp.concatenate([column, column, couple])
    place = jnp.arange(2 * rows + 2, dtype=jnp.int32)
    group = place // rows
    edge = row * 2 // rows * (rows - 1)
    own = jnp.where(group == 2, edge, row) * 2 + jnp.where(group == 1, 1 - side, side)
    unit = jnp.where(group < 2, place % rows, jnp.where(place == 2 * rows, row, rows))
    matches = lists // leaves == own[:, None]
    position = jnp.arange(listed, dtype=jnp.int32)
    earlier = position[None, :] < position[:, None]
    same_leaf = position[None, :] // NB == position[:, None] // NB
    counted = matches[:, None, :]
    ranks = jnp.sum(counted & earlier, axis=2, dtype=jnp.int32)
    opens = jnp.sum(counted & earlier & same_leaf, axis=2, dtype=jnp.int32) == 0
    source = group[:, None] * leaves + lists % leaves
    target = unit[:, None] * leaves + position // NB
    wide = (rows + 1) * leaves
    values = (source * wide + target) * 2 + opens
    picked = chosen_entries(matches, ranks, values, leaves).reshape(-1)
    near = [picked // (2 * wide), picked // 2 % wide, picked % 2]
    leaf_of = position // NB
    leaf_ids = jnp.arange(leaves, dtype=jnp.int32)[:, None]
    upto = jnp.sum(counted & (leaf_of <= leaf_ids), axis=2, dtype=jnp.int32)
    some = jnp.any(counted & (leaf_of == leaf_ids), axis=2)
    ends = jnp.where(some, place[:, None] * leaves + upto, 0).reshape(-1)

    count = nodes * FAR
    peers = far_lists.reshape(rows, 2, count)
    pair = lax.dynamic_index_in_dim(peers, row, 0, keepdims=False)
    mine = lax.dynamic_index_in_dim(pair, side, 0, keepdims=False)
    beside = lax.dynamic_index_in_dim(pair, 1 - side, 0, keepdims=False)
    lists = jnp.stack([mine, beside])
    sides = jnp.stack([side, 1 - side])[:, None]
    owners = lists // nodes
    slot = (owners + sides) % 2 * rows + owners // 2
    entry = jnp.arange(count, dtype=jnp.int32)
    before = entry[None, :] < entry[:, None]
    rank = jnp.sum((slot[:, :, None] == slot[:, None, :]) & before, axis=2, dtype=jnp.int32)
    at = slot * leaves + rank
    wide = 2 * rows * leaves
    chosen = chosen_entries(jnp.full((2, count), True), at, lists % nodes * count + entry, wide)
    beside_picks = chosen[1, rows * leaves :] // count
    lines = near + [ends, chosen[0] // count, chosen[0] % count, at[0], beside_picks]
    longest = max(line.shape[0] for line in lines)
    return jnp.stack([jnp.pad(line, (0, longest - line.shape[0])) for line in lines])


def gathered(coords, rhs, basis, transfer_one, transfer_two, far_blocks, neighbours, far_lists):
    peer_count = lax.axis_size("leaf")
    parts = lax.axis_size("rhs")
    rows = peer_count // 2
    device_index = lax.axis_index("leaf")
    leaves, nodes = basis.shape[0], far_blocks.shape[0]
    table = route_tables(
        rows, leaves, nodes, device_index // 2, device_index % 2, neighbours, far_lists
    )
    smem = pl.BlockSpec(memory_space=pltpu.SMEM)
    anywhere = pl.BlockSpec(memory_space=pl.ANY)
    bf16, f32 = jnp.bfloat16, jnp.float32
    chunks = leaves // CHUNK
    dma = pltpu.SemaphoreType.DMA
    return pl.pallas_call(
        functools.partial(whole_kernel, rows, parts),
        out_shape=jax.ShapeDtypeStruct((R, rhs.shape[1]), f32),
        in_specs=[smem] + [anywhere] * 6,
        out_specs=pl.BlockSpec(memory_space=pltpu.VMEM),
        scratch_shapes=[
            pltpu.VMEM((leaves, FEAT, LEAF), bf16),
            pltpu.VMEM((leaves, FEAT, LEAF), bf16),
            pltpu.VMEM((rows, leaves, FEAT, LEAF), bf16),
            pltpu.VMEM((leaves, R, LEAF), bf16),
            pltpu.VMEM((leaves, R, LEAF), bf16),
            pltpu.VMEM((leaves, R, LEAF), bf16),
            pltpu.VMEM((leaves, R, LEAF), bf16),
            pltpu.VMEM((leaves, R, LEAF), bf16),
            pltpu.VMEM((rows, nodes, R, RANK), bf16),
            pltpu.VMEM((rows, leaves, R, RANK), bf16),
            pltpu.VMEM((rows, leaves, R, RANK), bf16),
            pltpu.VMEM((rows, leaves, R, LEAF), bf16),
            pltpu.VMEM((2, rows, leaves, R, LEAF), bf16),
            pltpu.VMEM((3 * leaves, FEAT + AUG, LEAF), bf16),
            pltpu.VMEM(((rows + 1) * leaves, FEAT + AUG, LEAF), bf16),
            pltpu.VMEM((3 * leaves, R, LEAF), bf16),
            pltpu.VMEM((nodes, R, RANK), bf16),
            pltpu.VMEM(((peer_count + 2) * leaves + 1, R, LEAF), f32),
            pltpu.VMEM((peer_count * leaves, R, RANK), f32),
            pltpu.VMEM((nodes, R, RANK), f32),
            pltpu.VMEM(basis.shape, bf16),
            pltpu.VMEM(transfer_one.shape, bf16),
            pltpu.VMEM(transfer_two.shape, bf16),
            pltpu.VMEM((nodes * FAR, RANK, RANK), bf16),
            dma((4,)),
            dma((2, leaves)),
            dma((rows, 2)),
            dma((rows,)),
            dma((rows + 1, 3)),
            dma((rows + 1, 3)),
            dma((rows, 3, 2)),
            dma((rows, 3)),
            dma((rows, chunks)),
            dma((2, rows, chunks)),
            dma((3,)),
            dma((3,)),
            dma((rows,)),
            dma((rows,)),
            dma((1,)),
            dma((1,)),
        ],
        compiler_params=pltpu.CompilerParams(
            collective_id=0, has_side_effects=True, vmem_limit_bytes=60 * 1024 * 1024
        ),
        name="whole",
    )(
        table, coords, rhs, basis, transfer_one, transfer_two,
        far_blocks.reshape(nodes * FAR, RANK, RANK),
    )


def solution(mesh):
    return jax.shard_map(
        on_device,
        mesh=mesh,
        in_specs=(
            P(None, "leaf"),
            P("rhs", "leaf"),
            P("leaf", None, None),
            P("leaf", None, None),
            P("leaf", None, None),
            P("leaf", None, None, None),
            P(),
            P(),
        ),
        out_specs=P("rhs", "leaf"),
        check_vma=False,
    )
```
